128 devices in a mesh: seq: 32 (over y, z, core), head: 4 (over x).
Axes of the slice: x: 4, y: 4, z: 4, core: 2. Of those that a mesh axis runs over, the one named last changes fastest.
Arguments:
- hidden: bfloat16 [16384, 4096], P('seq'), may hold values from -6 to 6
- positions: int32 [16384], P('seq'), may hold values from 0 to 3342335, as said below
- w_x: bfloat16 [4096, 4096], P('seq', 'head'), may hold values from -0.09375 to 0.09375
- w_bc: bfloat16 [4096, 1024], P('seq', 'head'), may hold values from -0.0078125 to 0.0078125
- w_dt: bfloat16 [4096, 64], P('seq', 'head'), may hold values from -0.09375 to 0.09375
- a_log: float32 [64], P('head'), may hold values from -10 to -4
- dt_bias: float32 [64], P('head'), may hold values from -1 to 1
- d_skip: float32 [64], P('head'), may hold values from 0.5 to 1.5
- grad_out: bfloat16 [16384, 4096], P('seq', 'head'), may hold values from -6 to 6
Outputs:
- d_hidden: bfloat16 [16384, 4096], P('seq', 'head')
- d_w_x: bfloat16 [4096, 4096], P('seq', 'head')
- d_w_bc: bfloat16 [4096, 1024], P('seq', 'head')
- d_w_dt: bfloat16 [4096, 64], P('seq', 'head')
- d_head_params: float32 [3, 64], P(None, 'head')
The draws below stay inside these ranges and needn't reach their ends.
Inputs may be any that keep to these rules, and one draw needn't show every extreme that they name: positions rise strictly from token to token.
All inputs are finite; a program needn't handle non-finite values.
Results may differ from the reference program's by a relative error of at most 0.034.
Values may be sent and summed in bfloat16 or wider, within the bound.
A program may use at most 192 MiB of HBM per device.

```python
import jax
import jax.numpy as jnp
from jax import lax

D = 4096
HEAD_DIM = 64
STATE = 128
HEADS = 64
SPAN = 256
TOK_DEV = 512
RETAINED_ITEMS = 16384
STATE_GROUPS = 4
N_SEQ = 32


def draw_positions(key, part):
    first_key, alternate_seed_handle = jax.random.split(jax.random.fold_in(key, 17))
    spacing_jumps = jax.random.randint(first_key, (RETAINED_ITEMS,), 1, 5)
    contiguous_runs_extent = jax.random.randint(alternate_seed_handle, (RETAINED_ITEMS,), 0, 256)
    spacing_jumps = spacing_jumps + jnp.where(contiguous_runs_extent == 0, 200, 0)
    placed = (jnp.cumsum(spacing_jumps) - 1).astype(jnp.int32)
    return placed.at[RETAINED_ITEMS - 1].set(204 * RETAINED_ITEMS - 1)


def shard_levels(stream_key, shape, cuts, smallest, top_value):
    loudness, own = 1.0, jax.random.fold_in(stream_key, 6)
    for axis_at, shards_of in cuts:
        heights = jnp.exp(jax.random.uniform(jax.random.fold_in(own, axis_at), (shards_of,), jnp.float32, smallest / len(cuts), top_value / len(cuts)))
        loudness = loudness * jnp.repeat(heights, shape[axis_at] // shards_of).reshape([-1 if axis == axis_at else 1 for axis in range(len(shape))])
    return loudness


def bell_draw(rng, shape, width, reach, shards=(), held_as=jnp.bfloat16):
    array = jax.random.normal(rng, shape, jnp.float32) * width
    if len(shards) > 0:
        array = shard_levels(rng, shape, shards, -0.22, 0.18) * array
    return jnp.clip(array, min=-reach, max=reach).astype(held_as)


def setup_inputs(seed: int = 0) -> dict:
    key_list = jax.random.split(jax.random.key(seed), 10)
    hidden = bell_draw(key_list[0], (RETAINED_ITEMS, D), 1.0, 6.0, ((0, 32),))
    positions = draw_positions(jax.random.fold_in(key_list[9], 71), 0)
    w_x = bell_draw(key_list[2], (D, HEADS * HEAD_DIM), D ** -0.5, 0.09375, ((0, 32), (1, 4)))
    w_bc = bell_draw(key_list[3], (D, STATE_GROUPS * 2 * STATE), (D * STATE) ** -0.5, 0.0078125, ((0, 32), (1, 4)))
    w_dt = bell_draw(key_list[4], (D, HEADS), D ** -0.5, 0.09375, ((0, 32), (1, 4)))
    a_log = jnp.clip(-10.0 + 6.0 * jax.random.uniform(key_list[5], (HEADS,), jnp.float32) ** shard_levels(key_list[5], (HEADS,), ((0, 4),), -0.2, 0.2), -10.0, -4.0)
    dt_bias = jnp.clip(jax.random.uniform(key_list[6], (HEADS,), jnp.float32, -1.0, 1.0) * shard_levels(key_list[6], (HEADS,), ((0, 4),), -0.4, 0.0), -1.0, 1.0)
    d_skip = jnp.clip(0.5 + 1.0 * jax.random.uniform(key_list[7], (HEADS,), jnp.float32) ** shard_levels(key_list[7], (HEADS,), ((0, 4),), -0.2, 0.2), 0.5, 1.5)
    grad_out = bell_draw(key_list[8], (RETAINED_ITEMS, HEADS * HEAD_DIM), 1.0, 6.0, ((0, 32), (1, 4)))
    return dict(hidden=hidden, positions=positions, w_x=w_x, w_bc=w_bc, w_dt=w_dt, a_log=a_log, dt_bias=dt_bias, d_skip=d_skip, grad_out=grad_out)


exact_mode = lax.Precision.HIGHEST

def ssd_blocks(x_heads, input_matrix_mapping, c_proj, dt_heads, decay_log, initial, skip_gain, block_len):
    length, num_heads, head_dim = x_heads.shape
    num_groups = input_matrix_mapping.shape[1]
    state_len = input_matrix_mapping.shape[2]
    per_group = num_heads // num_groups
    block_list = length // block_len
    lower_mask = jnp.tril(jnp.ones((block_len, block_len), dtype=bool))

    def advance_raw(carry_state, pieces):
        x_blk, b_blk, c_blk, step_size_block, a_blk = pieces
        cum_decay = jnp.cumsum(a_blk, axis=0)
        by_head = cum_decay.T
        differ = by_head[:, :, None] - by_head[:, None, :]
        within = jnp.exp(jnp.where(lower_mask[None], differ, -jnp.inf))
        scores = jnp.einsum('tgn,sgn->gts', c_blk, b_blk, precision=exact_mode)
        scores_heads = jnp.repeat(scores, per_group, axis=0)
        b_heads = jnp.repeat(b_blk, per_group, axis=1)
        c_heads = jnp.repeat(c_blk, per_group, axis=1)
        mixing = within * scores_heads * step_size_block.T[:, None, :]
        intra_piece_output = jnp.einsum('hts,shp->thp', mixing, x_blk, precision=exact_mode)
        y_off = jnp.einsum('thn,hpn->thp', c_heads, carry_state, precision=exact_mode) * jnp.exp(cum_decay)[:, :, None]
        tail_weight = jnp.exp(cum_decay[-1][None, :] - cum_decay) * step_size_block
        fresh_part = jnp.einsum('sh,shp,shn->hpn', tail_weight, x_blk, b_heads, precision=exact_mode)
        next_state = jnp.exp(cum_decay[-1])[:, None, None] * carry_state + fresh_part
        outputs = intra_piece_output + y_off + skip_gain[None, :, None] * x_blk
        return (next_state, outputs)
    advance = jax.checkpoint(advance_raw)
    pieces = (x_heads.reshape(block_list, block_len, num_heads, head_dim), input_matrix_mapping.reshape(block_list, block_len, num_groups, state_len), c_proj.reshape(block_list, block_len, num_groups, state_len), dt_heads.reshape(block_list, block_len, num_heads), decay_log.reshape(block_list, block_len, num_heads))
    final_state, outputs = lax.scan(advance, initial, pieces)
    return (outputs.reshape(length, num_heads, head_dim), final_state)

def reference(hidden, positions, w_x, w_bc, w_dt, a_log, dt_bias, d_skip, grad_out):
    inner_width = w_x.shape[1]
    num_heads = w_dt.shape[1]
    state_len = STATE
    num_groups = w_bc.shape[1] // (2 * state_len)
    head_dim = inner_width // num_heads
    length = hidden.shape[0]
    x_pre = jnp.dot(hidden, w_x, preferred_element_type=jnp.float32)
    dt_pre = jnp.dot(hidden, w_dt, preferred_element_type=jnp.float32) + dt_bias[None, :]
    both_maps = jnp.dot(hidden, w_bc, preferred_element_type=jnp.float32).reshape(length, num_groups, 2, state_len)
    input_matrix_mapping = both_maps[:, :, 0, :]
    c_proj = both_maps[:, :, 1, :]
    x_heads = jax.nn.silu(x_pre).reshape(length, num_heads, head_dim)
    dt_heads = jax.nn.softplus(dt_pre)
    earlier_pos = jnp.concatenate([jnp.zeros((1,), jnp.int32), positions[:-1]])
    gap_len = (positions - earlier_pos).astype(jnp.float32)
    decay_rate = jnp.exp(a_log)
    decay_log = -decay_rate[None, :] * dt_heads * gap_len[:, None]
    initial = jnp.zeros((num_heads, head_dim, state_len), jnp.float32)

    def forward(x_in, b_in, c_in, dt_in, a_in, skip_in):
        return ssd_blocks(x_in, b_in, c_in, dt_in, a_in, initial, skip_in, SPAN)[0]
    outputs_fwd, pull = jax.vjp(forward, x_heads, input_matrix_mapping, c_proj, dt_heads, decay_log, d_skip)
    grad_heads = grad_out.astype(jnp.float32).reshape(length, num_heads, head_dim)
    grad_x, grad_b, readout_adjoint, grad_dt, grad_decay, grad_skip = pull(grad_heads)
    grad_dt_pre = (grad_dt - grad_decay * decay_rate[None, :] * gap_len[:, None]) * jax.nn.sigmoid(dt_pre)
    step_size_gradient_low = grad_dt_pre.astype(jnp.bfloat16)
    sig_x = jax.nn.sigmoid(x_pre)
    grad_x_pre = (grad_x.reshape(length, inner_width) * (sig_x + x_pre * sig_x * (1.0 - sig_x))).astype(jnp.bfloat16)
    state_grad = jnp.stack([grad_b, readout_adjoint], axis=2).reshape(length, num_groups * 2 * state_len).astype(jnp.bfloat16)
    contract = (((1,), (1,)), ((), ()))
    d_hidden = (lax.dot_general(grad_x_pre, w_x, contract, preferred_element_type=jnp.float32) + lax.dot_general(step_size_gradient_low, w_dt, contract, preferred_element_type=jnp.float32) + lax.dot_general(state_grad, w_bc, contract, preferred_element_type=jnp.float32)).astype(jnp.bfloat16)
    grad_cols = jnp.concatenate([grad_x_pre, step_size_gradient_low, state_grad], axis=1)

    def accumulate(running, index):
        first_row = (index * TOK_DEV).astype(jnp.int32)
        block_hidden = lax.dynamic_slice_in_dim(hidden, first_row, TOK_DEV, 0)
        block_grads = lax.dynamic_slice_in_dim(grad_cols, first_row, TOK_DEV, 0)
        term = lax.dot_general(block_hidden, block_grads, (((0,), (0,)), ((), ())), preferred_element_type=jnp.float32)
        rounded = lax.optimization_barrier(term.astype(jnp.bfloat16))
        return (running + rounded.astype(jnp.float32), None)
    start_sum = jnp.zeros((hidden.shape[1], grad_cols.shape[1]), jnp.float32)
    weight_grads = lax.scan(accumulate, start_sum, jnp.arange(N_SEQ, dtype=jnp.int32))[0]
    d_w_x = weight_grads[:, :inner_width].astype(jnp.bfloat16)
    d_w_dt = weight_grads[:, inner_width:inner_width + num_heads].astype(jnp.bfloat16)
    d_w_bc = weight_grads[:, inner_width + num_heads:].astype(jnp.bfloat16)
    d_head_params = jnp.stack([lax.optimization_barrier(jnp.sum(grad_decay * decay_log, axis=0)), lax.optimization_barrier(jnp.sum(grad_dt_pre, axis=0)), grad_skip])
    return (d_hidden, d_w_x, d_w_bc, d_w_dt, d_head_params)
```

```python
import functools

import jax
import jax.numpy as jnp
from jax import lax
from jax.experimental import pallas as pl
from jax.experimental.pallas import tpu as pltpu
from jax.sharding import PartitionSpec as P

STATE = 128
HEAD_DIM = 64
TILE = 256
LOG2E = 1.4426950408889634
MESH = pl.DeviceIdType.MESH
F32 = jnp.float32
BF16 = jnp.bfloat16
EXACT = lax.Precision.HIGHEST


def dot(a, b, dims, precision=None):
    return lax.dot_general(a, b, (dims, ((), ())), precision=precision, preferred_element_type=F32)


NN = ((1,), (0,))
NT = ((1,), (1,))
TN = ((0,), (0,))


def split2(v):
    hi = v.astype(BF16)
    return hi, (v - hi.astype(F32)).astype(BF16)


def split3(v):
    hi = v.astype(BF16)
    rest = v - hi.astype(F32)
    mid = rest.astype(BF16)
    return hi, mid, (rest - mid.astype(F32)).astype(BF16)


def spread(v, pick):
    parts = split3(v)
    return dot(jnp.concatenate(parts, axis=0), jnp.concatenate([pick] * 3, axis=0), TN)


def gather_heads(pick, y):
    hi, lo = split2(y)
    return dot(pick, hi, NT) + dot(pick, lo, NT)


def picker(heads, width):
    row = lax.broadcasted_iota(jnp.int32, (heads, heads * width), 0)
    col = lax.broadcasted_iota(jnp.int32, (heads, heads * width), 1)
    return jnp.where(col // width == row, 1.0, 0.0).astype(BF16)


def sigmoid(v):
    return 1.0 / (1.0 + jnp.exp(-v))


def scan_kernel(
    n,
    xp_ref,
    bc_ref,
    dtp_ref,
    gap_ref,
    rate_ref,
    skip_ref,
    g_ref,
    gcols_ref,
    gdt_ref,
    sums_ref,
    pay,
    got,
    back,
    home,
    decs,
    xs_ref,
    tail_ref,
    dtx_ref,
    xd_ref,
    xt_ref,
    ge_ref,
    u_ref,
    colb_ref,
    cumt_ref,
    cbt_ref,
    dcbt_ref,
    rowe_ref,
    cole_ref,
    send1,
    recv1,
    send2,
    recv2,
):
    tokens, width = xp_ref.shape
    heads = dtp_ref.shape[0]
    blocks = tokens // TILE
    piece = width // n
    me = lax.axis_index("seq")

    barrier = pltpu.get_barrier_semaphore()

    def greet(k, carry):
        pl.semaphore_signal(
            barrier, inc=1, device_id={"seq": lax.rem(me + k, n)}, device_id_type=MESH
        )
        return carry

    lax.fori_loop(1, n, greet, 0)

    pick = picker(heads, HEAD_DIM)
    dtp = dtp_ref[...]
    dt = jnp.maximum(dtp, 0.0) + jnp.log1p(jnp.exp(-jnp.abs(dtp)))
    rate = rate_ref[...]
    gap = gap_ref[...]
    decay = -rate * dt * gap
    before = lax.broadcasted_iota(jnp.int32, (tokens, tokens), 0)
    after = lax.broadcasted_iota(jnp.int32, (tokens, tokens), 1)
    upto = jnp.where(before <= after, 1.0, 0.0).astype(BF16)
    parts = jnp.concatenate(split3(decay * LOG2E), axis=0)
    raw = dot(parts, upto, NN)
    cum = raw[:heads] + raw[heads : 2 * heads] + raw[2 * heads :]
    cumt_ref[...] = cum
    last = cum[:, tokens - 1 :]
    whole = jnp.exp2(last)
    ecum = jnp.exp2(cum)
    tail = jnp.exp2(last - cum)

    colb_ref[...] = spread(cum, picker(heads, 128))
    dtx_ref[...] = spread(dt, pick)
    tail_ref[...] = spread(tail, pick)
    sums_skip = jnp.zeros((heads, 1), F32)
    for b in range(blocks):
        rows = pl.ds(b * TILE, TILE)
        xp = xp_ref[rows, :]
        xs = xp * sigmoid(xp)
        xs_ref[rows, :] = xs
        xd = xs * dtx_ref[rows, :]
        xd_ref[rows, :] = xd.astype(BF16)
        xt_ref[rows, :] = (xd * tail_ref[rows, :]).astype(BF16)
        g = g_ref[rows, :].astype(F32)
        ge_ref[rows, :] = (g * spread(ecum[:, b * TILE : (b + 1) * TILE], pick)).astype(BF16)
        sums_skip += jnp.sum(gather_heads(pick, g * xs), axis=1, keepdims=True)
    b_low = bc_ref[:, :STATE].astype(BF16)
    c_low = bc_ref[:, STATE:].astype(BF16)

    parts = split3(jnp.broadcast_to(whole, (heads, STATE)))
    for k in range(3):
        decs[k] = parts[k].astype(F32)
    local_state = dot(xt_ref[...], b_low, TN).astype(BF16)
    local_adjoint = dot(ge_ref[...], c_low, TN).astype(BF16)
    pay[:, :piece, :] = local_state.reshape(n, piece, STATE)
    pay[:, piece : 2 * piece, :] = local_adjoint.reshape(n, piece, STATE)
    which = lax.broadcasted_iota(jnp.int32, (16, STATE), 0)
    per_head = n // heads

    def fill(h, carry):
        one = [jnp.broadcast_to(decs[k, pl.ds(h, 1), :], (16, STATE)) for k in range(3)]
        block = jnp.where(which == 0, one[0], jnp.where(which == 1, one[1], one[2])).astype(BF16)
        for k in range(per_head):
            pay[h * per_head + k, 2 * piece :, :] = block
        return carry

    lax.fori_loop(0, heads, fill, 0)
    got[me] = pay[me]
    pl.semaphore_wait(barrier, n - 1)

    def out_copy(k):
        to = lax.rem(me + k, n)
        return pltpu.make_async_remote_copy(
            pay.at[to], got.at[me], send1.at[k], recv1.at[k], {"seq": to}, MESH
        )

    def start_out(k, carry):
        out_copy(k).start()
        return carry

    lax.fori_loop(1, n, start_out, 0)

    for i in range(blocks):
        for j in range(i, blocks):
            cbt_ref[i, j] = dot(
                b_low[i * TILE : (i + 1) * TILE], c_low[j * TILE : (j + 1) * TILE], NT
            )
            dcbt_ref[i, j] = jnp.zeros((TILE, TILE), F32)
    cole_ref[...] = jnp.zeros_like(cole_ref)
    s_at = lax.broadcasted_iota(jnp.int32, (TILE, TILE), 0)
    t_at = lax.broadcasted_iota(jnp.int32, (TILE, TILE), 1)
    lane = lax.broadcasted_iota(jnp.int32, (TILE, 128), 1)

    def pair(q, carry):
        cols = pl.ds(pl.multiple_of(q * 128, 128), 128)
        rowe = [[jnp.zeros((1, TILE), F32) for _ in range(blocks)] for _ in range(2)]
        for i in range(blocks):
            srows = pl.ds(i * TILE, TILE)
            xd = xd_ref[srows, cols]
            us = []
            for side in range(2):
                h = q * 2 + side
                lanes = slice(side * HEAD_DIM, (side + 1) * HEAD_DIM)
                col = colb_ref[srows, pl.ds(pl.multiple_of(h * 128, 128), 128)]
                col = jnp.concatenate([col] * (TILE // 128), axis=1)
                u = jnp.zeros((TILE, HEAD_DIM), F32)
                cole = jnp.zeros((TILE, 1), F32)
                for j in range(i, blocks):
                    g = g_ref[pl.ds(j * TILE, TILE), cols][:, lanes]
                    diff = cumt_ref[pl.ds(h, 1), pl.ds(j * TILE, TILE)] - col
                    if i == j:
                        diff = jnp.where(t_at >= s_at, diff, -jnp.inf)
                    within = jnp.exp2(diff)
                    f = within * dot(xd[:, lanes], g, NT)
                    dcbt_ref[i, j] += f
                    cb = cbt_ref[i, j]
                    e = cb * f
                    rowe[side][j] += jnp.sum(e, axis=0, keepdims=True)
                    cole += jnp.sum(e, axis=1, keepdims=True)
                    u += dot((within * cb).astype(BF16), g, NN)
                us.append(u)
                cole_ref[srows, :] = jnp.where(lane == h, cole, cole_ref[srows, :])
            u_ref[srows, cols] = jnp.concatenate(us, axis=1)
        for side in range(2):
            rowe_ref[pl.ds(q * 2 + side, 1), :] = jnp.concatenate(rowe[side], axis=1)
        return carry

    pairs = heads // 2
    lax.fori_loop(0, pairs // 2, pair, 0)

    def wait_out(k, carry):
        out_copy(k).wait_recv()
        return carry

    lax.fori_loop(1, n, wait_out, 0)

    def decay_of(d):
        rows = got[d, 2 * piece :, :].astype(F32)
        return rows[0:1] + rows[1:2] + rows[2:3]

    def ahead(d, state):
        back[d, :piece, :] = state.astype(BF16)
        return decay_of(d) * state + got[d, :piece, :].astype(F32)

    def behind(k, state):
        d = n - 1 - k
        back[d, piece:, :] = state.astype(BF16)
        return decay_of(d) * state + got[d, piece : 2 * piece, :].astype(F32)

    zero = jnp.zeros((piece, STATE), F32)
    lax.fori_loop(0, n, ahead, zero)
    lax.fori_loop(0, n, behind, zero)
    home[me] = back[me]

    def back_copy(k):
        to = lax.rem(me + k, n)
        return pltpu.make_async_remote_copy(
            back.at[to], home.at[me], send2.at[k], recv2.at[k], {"seq": to}, MESH
        )

    def start_back(k, carry):
        back_copy(k).start()
        return carry

    lax.fori_loop(1, n, start_back, 0)
    lax.fori_loop(pairs // 2, pairs, pair, 0)

    def wait_back(k, carry):
        back_copy(k).wait_recv()
        back_copy(k).wait_send()
        out_copy(k).wait_send()
        return carry

    lax.fori_loop(1, n, wait_back, 0)

    s_in = home[:, :piece, :].reshape(width, STATE)
    d_out = home[:, piece:, :].reshape(width, STATE)
    gcum = rowe_ref[...] - cole_ref[...].T[:heads]
    grad_dt_parts, r_parts, off_parts = [], [], []
    skipx = spread(jnp.broadcast_to(skip_ref[...], (heads, 128)), pick)[0:1]
    for b in range(blocks):
        rows = pl.ds(b * TILE, TILE)
        bb, cc = b_low[b * TILE : (b + 1) * TILE], c_low[b * TILE : (b + 1) * TILE]
        tq = tail_ref[rows, :] * dot(bb, d_out, NT)
        z = u_ref[rows, :] + tq
        xs = xs_ref[rows, :]
        grad_dt_parts.append(gather_heads(pick, xs * z))
        r_parts.append(gather_heads(pick, xs * tq))
        off_parts.append(gather_heads(pick, ge_ref[rows, :].astype(F32) * dot(cc, s_in, NT)))
        grad_x = dtx_ref[rows, :] * z + skipx * g_ref[rows, :].astype(F32)
        xp = xp_ref[rows, :]
        sig = sigmoid(xp)
        gcols_ref[rows, :width] = (grad_x * (sig + xp * sig * (1.0 - sig))).astype(BF16)
        grad_b = dot(xt_ref[rows, :], d_out, NN)
        grad_c = dot(ge_ref[rows, :], s_in, NN)
        for j in range(b, blocks):
            grad_b += dot(
                dcbt_ref[b, j].astype(BF16), c_low[j * TILE : (j + 1) * TILE], NN
            )
        for i in range(b + 1):
            grad_c += dot(
                dcbt_ref[i, b].astype(BF16), b_low[i * TILE : (i + 1) * TILE], TN
            )
        gcols_ref[rows, width : width + STATE] = grad_b.astype(BF16)
        gcols_ref[rows, width + STATE :] = grad_c.astype(BF16)
    grad_dt = jnp.concatenate(grad_dt_parts, axis=1)
    r = dt * jnp.concatenate(r_parts, axis=1)
    gcum += jnp.concatenate(off_parts, axis=1) - r
    both = jnp.sum(s_in.astype(F32) * d_out.astype(F32), axis=1, keepdims=True)
    both = jnp.broadcast_to(both, (width, 128))
    hi, lo = split2(both)
    both = (dot(pick, hi, NN) + dot(pick, lo, NN))[:, :1]
    at_end = jnp.sum(r, axis=1, keepdims=True) + whole * both
    parts = jnp.concatenate(split3(gcum), axis=0)
    raw = dot(parts, upto, NT)
    grad_decay = raw[:heads] + raw[heads : 2 * heads] + raw[2 * heads :] + at_end
    grad_dt_pre = (grad_dt - grad_decay * rate * gap) * sigmoid(dtp)
    gdt_ref[...] = grad_dt_pre.astype(BF16)
    slot = lax.broadcasted_iota(jnp.int32, (heads, 128), 1)
    sum_a = jnp.sum(grad_decay * decay, axis=1, keepdims=True)
    sum_b = jnp.sum(grad_dt_pre, axis=1, keepdims=True)
    sums_ref[...] = jnp.where(slot == 0, sum_a, jnp.where(slot == 1, sum_b, sums_skip))


def scan_call(n, xp, bc, dtp, gap, rate, skip, g):
    tokens, width = xp.shape
    heads = dtp.shape[0]
    blocks = tokens // TILE
    piece = width // n
    vm = pl.BlockSpec(memory_space=pltpu.VMEM)
    return pl.pallas_call(
        functools.partial(scan_kernel, n),
        name="scan",
        out_shape=(
            jax.ShapeDtypeStruct((tokens, width + 2 * STATE), BF16),
            jax.ShapeDtypeStruct((heads, tokens), BF16),
            jax.ShapeDtypeStruct((heads, 128), F32),
        ),
        in_specs=[vm] * 7,
        out_specs=(vm, vm, vm),
        scratch_shapes=[
            pltpu.VMEM((n, 2 * piece + 16, STATE), BF16),
            pltpu.VMEM((n, 2 * piece + 16, STATE), BF16),
            pltpu.VMEM((n, 2 * piece, STATE), BF16),
            pltpu.VMEM((n, 2 * piece, STATE), BF16),
            pltpu.VMEM((3, heads, STATE), F32),
            pltpu.VMEM((tokens, width), F32),
            pltpu.VMEM((tokens, width), F32),
            pltpu.VMEM((tokens, width), F32),
            pltpu.VMEM((tokens, width), BF16),
            pltpu.VMEM((tokens, width), BF16),
            pltpu.VMEM((tokens, width), BF16),
            pltpu.VMEM((tokens, width), F32),
            pltpu.VMEM((tokens, heads * 128), F32),
            pltpu.VMEM((heads, tokens), F32),
            pltpu.VMEM((blocks, blocks, TILE, TILE), F32),
            pltpu.VMEM((blocks, blocks, TILE, TILE), F32),
            pltpu.VMEM((heads, tokens), F32),
            pltpu.VMEM((tokens, 128), F32),
            pltpu.SemaphoreType.DMA((n,)),
            pltpu.SemaphoreType.DMA((n,)),
            pltpu.SemaphoreType.DMA((n,)),
            pltpu.SemaphoreType.DMA((n,)),
        ],
        compiler_params=pltpu.CompilerParams(
            collective_id=1, has_side_effects=True, vmem_limit_bytes=60 * 2**20
        ),
    )(xp, bc, dtp, gap, rate, skip, g)


def total_kernel(n, in_ref, out_ref, got, send, recv):
    me = lax.axis_index("seq")
    barrier = pltpu.get_barrier_semaphore()

    def greet(k, carry):
        pl.semaphore_signal(
            barrier, inc=1, device_id={"seq": lax.rem(me + k, n)}, device_id_type=MESH
        )
        return carry

    lax.fori_loop(1, n, greet, 0)
    pl.semaphore_wait(barrier, n - 1)

    def copy(k):
        to = lax.rem(me + k, n)
        return pltpu.make_async_remote_copy(
            in_ref, got.at[me], send.at[k], recv.at[k], {"seq": to}, MESH
        )

    def start(k, carry):
        copy(k).start()
        return carry

    lax.fori_loop(1, n, start, 0)
    got[me] = in_ref[...]

    def wait(k, carry):
        copy(k).wait()
        return carry

    lax.fori_loop(1, n, wait, 0)
    out_ref[...] = jnp.sum(got[...], axis=0)


def total_call(n, value):
    vm = pl.BlockSpec(memory_space=pltpu.VMEM)
    return pl.pallas_call(
        functools.partial(total_kernel, n),
        name="total",
        out_shape=jax.ShapeDtypeStruct(value.shape, value.dtype),
        in_specs=[vm],
        out_specs=vm,
        scratch_shapes=[
            pltpu.VMEM((n,) + value.shape, value.dtype),
            pltpu.SemaphoreType.DMA((n,)),
            pltpu.SemaphoreType.DMA((n,)),
        ],
        compiler_params=pltpu.CompilerParams(collective_id=2, has_side_effects=True),
    )(value)


def body(n, hidden, positions, w_x, w_bc, w_dt, a_log, dt_bias, d_skip, grad_out):
    inner = w_x.shape[1]
    heads = w_dt.shape[1]
    maps = w_bc.shape[1]
    w_local = jnp.concatenate([w_x, w_bc, w_dt], axis=1)
    w_all = lax.all_gather(w_local, "seq", axis=0, tiled=True)
    projected = jnp.dot(hidden, w_all, preferred_element_type=F32)
    dtp = projected[:, inner + maps :].T + dt_bias[:, None]
    pairs = [(i, i + 1) for i in range(n - 1)]
    earlier = lax.ppermute(positions[-1:], "seq", pairs)
    gap = (positions - jnp.concatenate([earlier, positions[:-1]])).astype(F32)[None, :]
    rate = jnp.exp(a_log)[:, None]
    gcols, gdt, sums = scan_call(
        n,
        projected[:, :inner],
        projected[:, inner : inner + maps],
        dtp,
        gap,
        rate,
        d_skip[:, None],
        grad_out,
    )
    totals = total_call(n, sums)
    d_head_params = totals[:, :3].T
    grad_cols = jnp.concatenate([gcols, gdt.T], axis=1)
    hidden_terms = lax.dot_general(
        grad_cols, w_all, (((1,), (1,)), ((), ())), preferred_element_type=F32
    )
    d_hidden = lax.psum_scatter(
        hidden_terms.astype(BF16), "head", scatter_dimension=1, tiled=True
    )
    weight_grads = lax.psum_scatter(
        lax.dot_general(
            hidden, grad_cols, (((0,), (0,)), ((), ())), preferred_element_type=F32
        ).astype(BF16),
        "seq",
        scatter_dimension=0,
        tiled=True,
    )
    return (
        d_hidden,
        weight_grads[:, :inner],
        weight_grads[:, inner : inner + maps],
        weight_grads[:, inner + maps :],
        d_head_params,
    )


def solution(mesh):
    return jax.shard_map(
        functools.partial(body, mesh.shape["seq"]),
        mesh=mesh,
        in_specs=(
            P("seq", None),
            P("seq"),
            P("seq", "head"),
            P("seq", "head"),
            P("seq", "head"),
            P("head"),
            P("head"),
            P("head"),
            P("seq", "head"),
        ),
        out_specs=(
            P("seq", "head"),
            P("seq", "head"),
            P("seq", "head"),
            P("seq", "head"),
            P(None, "head"),
        ),
        check_vma=False,
    )
```

```python
import functools

import jax
import jax.numpy as jnp
from jax import lax
from jax.experimental import pallas as pl
from jax.experimental.pallas import tpu as pltpu
from jax.sharding import PartitionSpec as P

STATE = 128
HEAD_DIM = 64
TILE = 256
LOG2E = 1.4426950408889634
MESH = pl.DeviceIdType.MESH
F32 = jnp.float32
BF16 = jnp.bfloat16
EXACT = lax.Precision.HIGHEST


def dot(a, b, dims, precision=None):
    return lax.dot_general(a, b, (dims, ((), ())), precision=precision, preferred_element_type=F32)


NN = ((1,), (0,))
NT = ((1,), (1,))
TN = ((0,), (0,))


def split2(v):
    hi = v.astype(BF16)
    return hi, (v - hi.astype(F32)).astype(BF16)


def split3(v):
    hi = v.astype(BF16)
    rest = v - hi.astype(F32)
    mid = rest.astype(BF16)
    return hi, mid, (rest - mid.astype(F32)).astype(BF16)


def spread(v, pick):
    parts = split3(v)
    return dot(jnp.concatenate(parts, axis=0), jnp.concatenate([pick] * 3, axis=0), TN)


def gather_heads(pick, y):
    hi, lo = split2(y)
    return dot(pick, hi, NT) + dot(pick, lo, NT)


def picker(heads, width):
    row = lax.broadcasted_iota(jnp.int32, (heads, heads * width), 0)
    col = lax.broadcasted_iota(jnp.int32, (heads, heads * width), 1)
    return jnp.where(col // width == row, 1.0, 0.0).astype(BF16)


def sigmoid(v):
    return 1.0 / (1.0 + jnp.exp(-v))


def scan_kernel(
    n,
    pr_ref,
    dtp_ref,
    gap_ref,
    rate_ref,
    skip_ref,
    g_ref,
    gcols_ref,
    gdt_ref,
    sums_ref,
    pay,
    got,
    back,
    home,
    decs,
    xs_ref,
    tail_ref,
    dtx_ref,
    xd_ref,
    xt_ref,
    ge_ref,
    u_ref,
    colb_ref,
    cumt_ref,
    cbt_ref,
    dcbt_ref,
    rowe_ref,
    cole_ref,
    send1,
    recv1,
    send2,
    recv2,
):
    tokens = pr_ref.shape[0]
    width = pr_ref.shape[1] - 2 * STATE
    heads = dtp_ref.shape[0]
    blocks = tokens // TILE
    piece = width // n
    me = lax.axis_index("seq")

    barrier = pltpu.get_barrier_semaphore()

    def greet(k, carry):
        pl.semaphore_signal(
            barrier, inc=1, device_id={"seq": lax.rem(me + k, n)}, device_id_type=MESH
        )
        return carry

    lax.fori_loop(1, n, greet, 0)

    pick = picker(heads, HEAD_DIM)
    dtp = dtp_ref[...]
    dt = jnp.maximum(dtp, 0.0) + jnp.log1p(jnp.exp(-jnp.abs(dtp)))
    rate = rate_ref[...]
    gap = gap_ref[...]
    decay = -rate * dt * gap
    before = lax.broadcasted_iota(jnp.int32, (tokens, tokens), 0)
    after = lax.broadcasted_iota(jnp.int32, (tokens, tokens), 1)
    upto = jnp.where(before <= after, 1.0, 0.0).astype(BF16)
    parts = jnp.concatenate(split3(decay * LOG2E), axis=0)
    raw = dot(parts, upto, NN)
    cum = raw[:heads] + raw[heads : 2 * heads] + raw[2 * heads :]
    cumt_ref[...] = cum
    last = cum[:, tokens - 1 :]
    whole = jnp.exp2(last)
    ecum = jnp.exp2(cum)
    tail = jnp.exp2(last - cum)

    colb_ref[...] = spread(cum, picker(heads, 128))
    dtx_ref[...] = spread(dt, pick)
    tail_ref[...] = spread(tail, pick)
    sums_skip = jnp.zeros((heads, 1), F32)
    for b in range(blocks):
        rows = pl.ds(b * TILE, TILE)
        xp = pr_ref[rows, :width]
        xs = xp * sigmoid(xp)
        xs_ref[rows, :] = xs
        xd = xs * dtx_ref[rows, :]
        xd_ref[rows, :] = xd.astype(BF16)
        xt_ref[rows, :] = (xd * tail_ref[rows, :]).astype(BF16)
        g = g_ref[rows, :].astype(F32)
        ge_ref[rows, :] = (g * spread(ecum[:, b * TILE : (b + 1) * TILE], pick)).astype(BF16)
        sums_skip += jnp.sum(gather_heads(pick, g * xs), axis=1, keepdims=True)
    b_low = pr_ref[:, width : width + STATE].astype(BF16)
    c_low = pr_ref[:, width + STATE :].astype(BF16)

    parts = split3(jnp.broadcast_to(whole, (heads, STATE)))
    for k in range(3):
        decs[k] = parts[k].astype(F32)
    local_state = dot(xt_ref[...], b_low, TN).astype(BF16)
    local_adjoint = dot(ge_ref[...], c_low, TN).astype(BF16)
    pay[:, :piece, :] = local_state.reshape(n, piece, STATE)
    pay[:, piece : 2 * piece, :] = local_adjoint.reshape(n, piece, STATE)
    which = lax.broadcasted_iota(jnp.int32, (16, STATE), 0)
    per_head = n // heads

    def fill(h, carry):
        one = [jnp.broadcast_to(decs[k, pl.ds(h, 1), :], (16, STATE)) for k in range(3)]
        block = jnp.where(which == 0, one[0], jnp.where(which == 1, one[1], one[2])).astype(BF16)
        for k in range(per_head):
            pay[h * per_head + k, 2 * piece :, :] = block
        return carry

    lax.fori_loop(0, heads, fill, 0)
    got[me] = pay[me]
    pl.semaphore_wait(barrier, n - 1)

    def out_copy(k):
        to = lax.rem(me + k, n)
        return pltpu.make_async_remote_copy(
            pay.at[to], got.at[me], send1.at[k], recv1.at[k], {"seq": to}, MESH
        )

    def start_out(k, carry):
        out_copy(k).start()
        return carry

    lax.fori_loop(1, n, start_out, 0)

    for i in range(blocks):
        for j in range(i, blocks):
            cbt_ref[i, j] = dot(
                b_low[i * TILE : (i + 1) * TILE], c_low[j * TILE : (j + 1) * TILE], NT
            )
            dcbt_ref[i, j] = jnp.zeros((TILE, TILE), F32)
    cole_ref[...] = jnp.zeros_like(cole_ref)
    s_at = lax.broadcasted_iota(jnp.int32, (TILE, TILE), 0)
    t_at = lax.broadcasted_iota(jnp.int32, (TILE, TILE), 1)
    lane = lax.broadcasted_iota(jnp.int32, (TILE, 128), 1)

    def pair(q, carry):
        cols = pl.ds(pl.multiple_of(q * 128, 128), 128)
        rowe = [[jnp.zeros((1, TILE), F32) for _ in range(blocks)] for _ in range(2)]
        for i in range(blocks):
            srows = pl.ds(i * TILE, TILE)
            xd = xd_ref[srows, cols]
            us = []
            for side in range(2):
                h = q * 2 + side
                lanes = slice(side * HEAD_DIM, (side + 1) * HEAD_DIM)
                col = colb_ref[srows, pl.ds(pl.multiple_of(h * 128, 128), 128)]
                col = jnp.concatenate([col] * (TILE // 128), axis=1)
                u = jnp.zeros((TILE, HEAD_DIM), F32)
                cole = jnp.zeros((TILE, 1), F32)
                for j in range(i, blocks):
                    g = g_ref[pl.ds(j * TILE, TILE), cols][:, lanes]
                    diff = cumt_ref[pl.ds(h, 1), pl.ds(j * TILE, TILE)] - col
                    if i == j:
                        diff = jnp.where(t_at >= s_at, diff, -jnp.inf)
                    within = jnp.exp2(diff)
                    f = within * dot(xd[:, lanes], g, NT)
                    dcbt_ref[i, j] += f
                    cb = cbt_ref[i, j]
                    e = cb * f
                    rowe[side][j] += jnp.sum(e, axis=0, keepdims=True)
                    cole += jnp.sum(e, axis=1, keepdims=True)
                    u += dot((within * cb).astype(BF16), g, NN)
                us.append(u)
                cole_ref[srows, :] = jnp.where(lane == h, cole, cole_ref[srows, :])
            u_ref[srows, cols] = jnp.concatenate(us, axis=1)
        for side in range(2):
            rowe_ref[pl.ds(q * 2 + side, 1), :] = jnp.concatenate(rowe[side], axis=1)
        return carry

    pairs = heads // 2
    lax.fori_loop(0, pairs // 2, pair, 0)

    def wait_out(k, carry):
        out_copy(k).wait_recv()
        return carry

    lax.fori_loop(1, n, wait_out, 0)

    def decay_of(d):
        rows = got[d, 2 * piece :, :].astype(F32)
        return rows[0:1] + rows[1:2] + rows[2:3]

    def ahead(d, state):
        back[d, :piece, :] = state.astype(BF16)
        return decay_of(d) * state + got[d, :piece, :].astype(F32)

    def behind(k, state):
        d = n - 1 - k
        back[d, piece:, :] = state.astype(BF16)
        return decay_of(d) * state + got[d, piece : 2 * piece, :].astype(F32)

    zero = jnp.zeros((piece, STATE), F32)
    lax.fori_loop(0, n, ahead, zero)
    lax.fori_loop(0, n, behind, zero)
    home[me] = back[me]

    def back_copy(k):
        to = lax.rem(me + k, n)
        return pltpu.make_async_remote_copy(
            back.at[to], home.at[me], send2.at[k], recv2.at[k], {"seq": to}, MESH
        )

    def start_back(k, carry):
        back_copy(k).start()
        return carry

    lax.fori_loop(1, n, start_back, 0)
    lax.fori_loop(pairs // 2, pairs, pair, 0)

    def wait_back(k, carry):
        back_copy(k).wait_recv()
        back_copy(k).wait_send()
        out_copy(k).wait_send()
        return carry

    lax.fori_loop(1, n, wait_back, 0)

    s_in = home[:, :piece, :].reshape(width, STATE)
    d_out = home[:, piece:, :].reshape(width, STATE)
    gcum = rowe_ref[...] - cole_ref[...].T[:heads]
    grad_dt_parts, r_parts, off_parts = [], [], []
    skipx = spread(jnp.broadcast_to(skip_ref[...], (heads, 128)), pick)[0:1]
    for b in range(blocks):
        rows = pl.ds(b * TILE, TILE)
        bb, cc = b_low[b * TILE : (b + 1) * TILE], c_low[b * TILE : (b + 1) * TILE]
        tq = tail_ref[rows, :] * dot(bb, d_out, NT)
        z = u_ref[rows, :] + tq
        xs = xs_ref[rows, :]
        grad_dt_parts.append(gather_heads(pick, xs * z))
        r_parts.append(gather_heads(pick, xs * tq))
        off_parts.append(gather_heads(pick, ge_ref[rows, :].astype(F32) * dot(cc, s_in, NT)))
        grad_x = dtx_ref[rows, :] * z + skipx * g_ref[rows, :].astype(F32)
        xp = pr_ref[rows, :width]
        sig = sigmoid(xp)
        gcols_ref[rows, :width] = (grad_x * (sig + xp * sig * (1.0 - sig))).astype(BF16)
        grad_b = dot(xt_ref[rows, :], d_out, NN)
        grad_c = dot(ge_ref[rows, :], s_in, NN)
        for j in range(b, blocks):
            grad_b += dot(
                dcbt_ref[b, j].astype(BF16), c_low[j * TILE : (j + 1) * TILE], NN
            )
        for i in range(b + 1):
            grad_c += dot(
                dcbt_ref[i, b].astype(BF16), b_low[i * TILE : (i + 1) * TILE], TN
            )
        gcols_ref[rows, width : width + STATE] = grad_b.astype(BF16)
        gcols_ref[rows, width + STATE :] = grad_c.astype(BF16)
    grad_dt = jnp.concatenate(grad_dt_parts, axis=1)
    r = dt * jnp.concatenate(r_parts, axis=1)
    gcum += jnp.concatenate(off_parts, axis=1) - r
    both = jnp.sum(s_in.astype(F32) * d_out.astype(F32), axis=1, keepdims=True)
    both = jnp.broadcast_to(both, (width, 128))
    hi, lo = split2(both)
    both = (dot(pick, hi, NN) + dot(pick, lo, NN))[:, :1]
    at_end = jnp.sum(r, axis=1, keepdims=True) + whole * both
    parts = jnp.concatenate(split3(gcum), axis=0)
    raw = dot(parts, upto, NT)
    grad_decay = raw[:heads] + raw[heads : 2 * heads] + raw[2 * heads :] + at_end
    grad_dt_pre = (grad_dt - grad_decay * rate * gap) * sigmoid(dtp)
    gdt_ref[...] = grad_dt_pre.astype(BF16)
    slot = lax.broadcasted_iota(jnp.int32, (heads, 128), 1)
    sum_a = jnp.sum(grad_decay * decay, axis=1, keepdims=True)
    sum_b = jnp.sum(grad_dt_pre, axis=1, keepdims=True)
    sums_ref[...] = jnp.where(slot == 0, sum_a, jnp.where(slot == 1, sum_b, sums_skip))


def scan_call(n, proj, dtp, gap, rate, skip, g):
    tokens, width = g.shape
    heads = dtp.shape[0]
    blocks = tokens // TILE
    piece = width // n
    vm = pl.BlockSpec(memory_space=pltpu.VMEM)
    return pl.pallas_call(
        functools.partial(scan_kernel, n),
        name="scan",
        out_shape=(
            jax.ShapeDtypeStruct((tokens, width + 2 * STATE), BF16),
            jax.ShapeDtypeStruct((heads, tokens), BF16),
            jax.ShapeDtypeStruct((heads, 128), F32),
        ),
        in_specs=[vm] * 6,
        out_specs=(vm, vm, vm),
        scratch_shapes=[
            pltpu.VMEM((n, 2 * piece + 16, STATE), BF16),
            pltpu.VMEM((n, 2 * piece + 16, STATE), BF16),
            pltpu.VMEM((n, 2 * piece, STATE), BF16),
            pltpu.VMEM((n, 2 * piece, STATE), BF16),
            pltpu.VMEM((3, heads, STATE), F32),
            pltpu.VMEM((tokens, width), F32),
            pltpu.VMEM((tokens, width), F32),
            pltpu.VMEM((tokens, width), F32),
            pltpu.VMEM((tokens, width), BF16),
            pltpu.VMEM((tokens, width), BF16),
            pltpu.VMEM((tokens, width), BF16),
            pltpu.VMEM((tokens, width), F32),
            pltpu.VMEM((tokens, heads * 128), F32),
            pltpu.VMEM((heads, tokens), F32),
            pltpu.VMEM((blocks, blocks, TILE, TILE), F32),
            pltpu.VMEM((blocks, blocks, TILE, TILE), F32),
            pltpu.VMEM((heads, tokens), F32),
            pltpu.VMEM((tokens, 128), F32),
            pltpu.SemaphoreType.DMA((n,)),
            pltpu.SemaphoreType.DMA((n,)),
            pltpu.SemaphoreType.DMA((n,)),
            pltpu.SemaphoreType.DMA((n,)),
        ],
        compiler_params=pltpu.CompilerParams(
            collective_id=1, has_side_effects=True, vmem_limit_bytes=60 * 2**20
        ),
    )(proj, dtp, gap, rate, skip, g)


SIDE = 4


def row_of(r):
    return lax.rem(3 * (r + (r // 2) * (1 - 2 * lax.rem(r, 2))), SIDE)


def place(n):
    me = lax.axis_index("seq")
    core = lax.rem(me, 2)
    chip = me // 2
    y, z = chip // SIDE, lax.rem(chip, SIDE)
    p = y * (1 - core) + z * core
    q = z * (1 - core) + y * core

    def chip_at(dp, dq):
        return lax.rem(p + dp, SIDE) * (SIDE - (SIDE - 1) * core) + lax.rem(q + dq, SIDE) * (
            1 + (SIDE - 1) * core
        )

    return me, core, chip_at


def greet_all(barrier, ids):
    for axis, to in ids:
        pl.semaphore_signal(barrier, inc=1, device_id={axis: to}, device_id_type=MESH)


def eye(size):
    row = lax.broadcasted_iota(jnp.int32, (size, size), 0)
    col = lax.broadcasted_iota(jnp.int32, (size, size), 1)
    return jnp.where(row == col, 1.0, 0.0).astype(BF16)


def gather_kernel(
    n, cut, hid_hbm, wx_ref, wbc_ref, wdt_ref, bias_ref, proj_ref, dtp_ref, w_hbm, wall, hid, send, recv, local
):
    me, core, chip_at = place(n)
    partner = me + 1 - 2 * core
    inner, maps = wx_ref.shape[1], wbc_ref.shape[1]
    wide = inner + maps
    rows_all = wide + wdt_ref.shape[1]

    def sid(dp, dq):
        return 2 * chip_at(dp, dq) + core

    barrier = pltpu.get_barrier_semaphore()
    to_p = (sid(1, 0), sid(3, 0))
    to_q = (sid(0, 1), sid(0, 3))
    greet_all(barrier, [("seq", d) for d in to_p + to_q + (partner,)])
    load = pltpu.make_async_copy(hid_hbm, hid, local.at[n // 2])
    load.start()
    wall[me, :inner, :] = wx_ref[...].T
    wall[me, inner:wide, :] = wbc_ref[...].T
    wall[me, wide:, :] = dot(wdt_ref[...], eye(128), TN).astype(BF16)
    halves = (pl.ds(0, cut), pl.ds(cut, rows_all - cut))
    pl.semaphore_wait(barrier, 5)

    def copy(slot, half, to, sem):
        ref = wall.at[slot, halves[half]]
        return pltpu.make_async_remote_copy(
            ref, ref, send.at[sem], recv.at[2 * slot + half], {"seq": to}, MESH
        )

    sent = []

    def push(slot, half, to):
        c = copy(slot, half, to, len(sent))
        c.start()
        sent.append(c)

    def arrive(slot, half):
        copy(slot, half, partner, 0).wait_recv()

    for half in range(2):
        push(me, half, to_q[0])
        push(me, 1 - half, to_q[1])
        push(me, half, to_p[0])
        push(me, 1 - half, to_p[1])
    for half in range(2):
        push(me, half, partner)

    def along_q(slot, half):
        push(slot, half, to_q[0])
        push(slot, half, to_q[1])
        push(slot, half, partner)

    for dp, half, forward in ((3, 0, 0), (1, 1, 1), (3, 1, None), (1, 0, None)):
        slot = sid(dp, 0)
        arrive(slot, half)
        if forward is not None:
            push(slot, half, to_p[forward])
        along_q(slot, half)

    base = 30

    def round_copies(r):
        dp = row_of(r)
        out = []
        for i, (dq, half, forward) in enumerate(
            ((3, 0, 0), (1, 1, 1), (3, 1, None), (1, 0, None), (2, 0, None), (2, 1, None))
        ):
            slot = sid(dp, dq)
            some = []
            if forward is not None:
                some.append(copy(slot, half, to_q[forward], base + r * 8 + 6 + forward))
            some.append(copy(slot, half, partner, base + r * 8 + i))
            out.append((slot, half, some))
        return out

    def out_copy(chip):
        return pltpu.make_async_copy(
            wall.at[pl.ds(2 * chip, 2)], w_hbm.at[pl.ds(2 * chip, 2)], local.at[chip]
        )

    def take(chip):
        other = 2 * chip + 1 - core
        for half in range(2):
            copy(other, half, partner, 0).wait_recv()
        out_copy(chip).start()
        a = hid[:, pl.ds(pl.multiple_of(chip * 256, 256), 256)]
        b = jnp.concatenate([wall[2 * chip], wall[2 * chip + 1]], axis=1)
        proj_ref[...] += dot(a, b[:wide], NT)
        dtp_ref[...] += dot(b[wide:], a, NT)

    def one_round(r, carry):
        for slot, half, some in round_copies(r):
            copy(slot, half, partner, 0).wait_recv()
            for c in some:
                c.start()

        def chips(k, carry):
            second = k // (r + 1)
            a = r * (1 - second) + (k - r - 1) * second
            b = k * (1 - second) + r * second
            take(chip_at(row_of(a), row_of(b)))
            return carry

        lax.fori_loop(0, 2 * r + 1, chips, 0)
        return carry

    proj_ref[...] = jnp.zeros_like(proj_ref)
    dtp_ref[...] = jnp.broadcast_to(bias_ref[...], dtp_ref.shape)
    load.wait()
    for half in range(2):
        slot = sid(2, 0)
        arrive(slot, half)
        along_q(slot, half)
    assert len(sent) == base
    lax.fori_loop(0, SIDE, one_round, 0)

    for c in sent:
        c.wait_send()

    def done(r, carry):
        for _, _, some in round_copies(r):
            for c in some:
                c.wait_send()
        return carry

    lax.fori_loop(0, SIDE, done, 0)

    def stored(k, carry):
        out_copy(k).wait()
        return carry

    lax.fori_loop(0, n // 2, stored, 0)


def gather_call(n, hidden, w_x, w_bc, w_dt, bias):
    tokens = hidden.shape[0]
    heads = w_dt.shape[1]
    wide = w_x.shape[1] + w_bc.shape[1]
    rows = wide + heads
    vm = pl.BlockSpec(memory_space=pltpu.VMEM)
    hbm = pl.BlockSpec(memory_space=pl.ANY)
    return pl.pallas_call(
        functools.partial(gather_kernel, n, wide // 2),
        name="gather",
        out_shape=(
            jax.ShapeDtypeStruct((tokens, wide), F32),
            jax.ShapeDtypeStruct((heads, tokens), F32),
            jax.ShapeDtypeStruct((n, rows, 128), BF16),
        ),
        in_specs=[hbm, vm, vm, vm, vm],
        out_specs=(vm, vm, hbm),
        scratch_shapes=[
            pltpu.VMEM((n, rows, 128), BF16),
            pltpu.VMEM(hidden.shape, BF16),
            pltpu.SemaphoreType.DMA((62,)),
            pltpu.SemaphoreType.DMA((2 * n,)),
            pltpu.SemaphoreType.DMA((n // 2 + 1,)),
        ],
        compiler_params=pltpu.CompilerParams(
            collective_id=3, has_side_effects=True, vmem_limit_bytes=60 * 2**20
        ),
    )(hidden, w_x, w_bc, w_dt, bias)


class Ring:
    def __init__(self, axis, ids, cut, total, send, recv, base):
        self.axis, self.ids, self.base = axis, ids, base
        self.send, self.recv = send, recv
        self.rows = (pl.ds(0, cut), pl.ds(cut, total - cut))

    def bind(self, blocks, rel, fin):
        self.blocks, self.rel, self.fin = blocks, rel, fin
        low, high = self.rows
        plan = (
            (2, low, rel.at[low], 0),
            (2, high, rel.at[high], 1),
            (1, high, fin.at[0, high], 0),
            (3, low, fin.at[1, low], 1),
            (1, low, fin.at[0, low], 0),
            (3, high, fin.at[1, high], 1),
        )
        self.copies = [
            pltpu.make_async_remote_copy(
                blocks[b].at[rows],
                dst,
                self.send.at[self.base + k],
                self.recv.at[self.base + k],
                {self.axis: self.ids[side]},
                MESH,
            )
            for k, (b, rows, dst, side) in enumerate(plan)
        ]
        return self

    def relay(self):
        for k, (b, rows) in enumerate(((1, self.rows[0]), (3, self.rows[1]))):
            self.copies[k].wait_recv()
            ref = self.blocks[b]
            ref[rows, :] = (ref[rows, :].astype(F32) + self.rel[rows, :].astype(F32)).astype(BF16)
            self.copies[4 + k].start()

    def final(self):
        for k in range(2, 6):
            self.copies[k].wait_recv()
        own = self.blocks[0][...].astype(F32)
        return own + self.fin[0].astype(F32) + self.fin[1].astype(F32)

    def drain(self):
        for c in self.copies:
            c.wait_send()


def scatter_kernel(
    n,
    cut,
    hid_hbm,
    w_hbm,
    g_ref,
    gdt_ref,
    sums_ref,
    dh_ref,
    dwx_ref,
    dwbc_ref,
    dwdt_ref,
    tot_ref,
    hid,
    w,
    gt,
    xbuf,
    xrel,
    xfin,
    mine,
    theirs,
    fromp,
    rel,
    fin,
    got,
    send_p,
    recv_p,
    send_r,
    recv_r,
    send_s,
    recv_s,
    local,
):
    me, core, chip_at = place(n)
    partner = me + 1 - 2 * core
    head = lax.axis_index("head")
    tokens, wide = g_ref.shape
    inner = dwx_ref.shape[1]
    rows_all = gt.shape[0]
    per = n // SIDE
    order = (2, 1, 3, 0)

    def sid(dp, dq):
        return 2 * chip_at(dp, dq) + core

    def at_head(d):
        return lax.rem(head + d, SIDE)

    barrier = pltpu.get_barrier_semaphore()
    x_ids = (at_head(1), at_head(3))

    def greet(k, carry):
        pl.semaphore_signal(
            barrier, inc=1, device_id={"seq": lax.rem(me + k, n)}, device_id_type=MESH
        )
        return carry

    lax.fori_loop(1, n, greet, 0)
    greet_all(barrier, [("head", d) for d in x_ids])

    def w_copy(d):
        part = pl.ds(at_head(d) * per, per)
        return pltpu.make_async_copy(w_hbm.at[part], w.at[part], local.at[d])

    w_copy(2).start()
    load = pltpu.make_async_copy(hid_hbm, hid, local.at[SIDE])
    load.start()
    for d in (1, 3, 0):
        w_copy(d).start()
    gt[:wide, :] = g_ref[...].T
    gt[wide:, :] = gdt_ref[...]

    x_ring = Ring("head", x_ids, tokens // 2, tokens, send_r, recv_r, 0).bind(
        [xbuf.at[d] for d in range(SIDE)], xrel, xfin
    )
    q_ids = (sid(0, 1), sid(0, 3))
    p_ids = (sid(1, 0), sid(3, 0))
    groups = {}
    for g, a in enumerate(order):
        groups[a] = Ring("seq", q_ids, cut, rows_all, send_r, recv_r, 6 + 6 * g).bind(
            [mine.at[a * SIDE + b] for b in range(SIDE)], rel.at[g], fin.at[g]
        )
    p_ring = Ring("seq", p_ids, cut, rows_all, send_r, recv_r, 30).bind(
        [mine.at[a * SIDE] for a in range(SIDE)], rel.at[SIDE], fin.at[SIDE]
    )

    def hidden_part(d):
        first = at_head(d) * per

        def one(k, carry):
            b = jnp.concatenate([w[first + 2 * k], w[first + 2 * k + 1]], axis=1)
            part = dot(g_ref[...], b[:wide], NN) + dot(gdt_ref[...], b[wide:], TN)
            xbuf[d, :, pl.ds(pl.multiple_of(k * 256, 256), 256)] = part.astype(BF16)
            return carry

        lax.fori_loop(0, per // 2, one, 0)

    def partner_copy(a, b):
        return pltpu.make_async_remote_copy(
            theirs.at[a * SIDE + b],
            fromp.at[b * SIDE + a],
            send_p.at[a * SIDE + b],
            recv_p.at[b * SIDE + a],
            {"seq": partner},
            MESH,
        )

    def weight_part(a, b):
        chip = chip_at(a, b)
        at = a * SIDE + b
        x = jnp.concatenate(
            [
                hid[:, pl.ds(pl.multiple_of(chip * 256 + 128 * core, 128), 128)],
                hid[:, pl.ds(pl.multiple_of(chip * 256 + 128 * (1 - core), 128), 128)],
            ],
            axis=1,
        )
        part = dot(gt[...], x, NN).astype(BF16)
        mine[at] = part[:, :128]
        theirs[at] = part[:, 128:]
        partner_copy(a, b).start()

    def offset(r):
        return row_of(SIDE - 1 - r)

    def weight_ring(r):
        left = SIDE - r

        def one(k, carry):
            second = k // left
            a = r * (1 - second) + (k - left + r + 1) * second
            b = (r + k) * (1 - second) + r * second
            weight_part(offset(a), offset(b))
            return carry

        lax.fori_loop(0, 2 * left - 1, one, 0)

    def pair_sums(r):
        a = order[r]

        def one(b, carry):
            at = a * SIDE + b
            partner_copy(b, a).wait_recv()
            mine[at] = (mine[at].astype(F32) + fromp[at].astype(F32)).astype(BF16)
            return carry

        lax.fori_loop(0, SIDE, one, 0)
        for k in range(4):
            groups[a].copies[k].start()

    def line_sum(r):
        a = order[r]
        mine[a * SIDE] = groups[a].final().astype(BF16)
        if a == 2:
            p_ring.copies[0].start()
            p_ring.copies[1].start()
        if a == 1:
            p_ring.copies[2].start()
        if a == 3:
            p_ring.copies[3].start()

    def sums_copy(k):
        to = lax.rem(me + k, n)
        return pltpu.make_async_remote_copy(
            sums_ref, got.at[me], send_s.at[k], recv_s.at[k], {"seq": to}, MESH
        )

    w_copy(2).wait()
    hidden_part(2)
    pl.semaphore_wait(barrier, n + 1)
    x_ring.copies[0].start()
    x_ring.copies[1].start()
    load.wait()
    weight_ring(0)
    pair_sums(0)
    w_copy(1).wait()
    w_copy(3).wait()
    hidden_part(1)
    x_ring.copies[2].start()
    hidden_part(3)
    x_ring.copies[3].start()
    weight_ring(1)
    pair_sums(1)
    groups[2].relay()
    weight_ring(2)
    x_ring.relay()
    pair_sums(2)
    weight_ring(3)
    groups[1].relay()
    pair_sums(3)
    line_sum(0)

    def start_sums(k, carry):
        sums_copy(k).start()
        return carry

    lax.fori_loop(1, n, start_sums, 0)
    got[me] = sums_ref[...]
    w_copy(0).wait()
    hidden_part(0)
    groups[3].relay()
    line_sum(1)
    groups[0].relay()
    line_sum(2)
    p_ring.relay()
    line_sum(3)

    def wait_sums(k, carry):
        sums_copy(k).wait()
        return carry

    lax.fori_loop(1, n, wait_sums, 0)
    tot_ref[...] = jnp.sum(got[...], axis=0)
    grads = p_ring.final()
    dwx_ref[...] = grads[:inner].T.astype(BF16)
    dwbc_ref[...] = grads[inner:wide].T.astype(BF16)
    dwdt_ref[...] = dot(grads[wide:].astype(BF16), eye(rows_all - wide), TN).astype(BF16)
    dh_ref[...] = x_ring.final().astype(BF16)
    x_ring.drain()
    p_ring.drain()
    for ring in groups.values():
        ring.drain()

    def drained(k, carry):
        partner_copy(k // SIDE, lax.rem(k, SIDE)).wait_send()
        return carry

    lax.fori_loop(0, SIDE * SIDE, drained, 0)


def scatter_call(n, hidden, w_all, gcols, gdt, sums):
    tokens, wide = gcols.shape
    heads = gdt.shape[0]
    maps = 2 * STATE
    inner = wide - maps
    rows = wide + heads
    per = hidden.shape[1] // SIDE
    vm = pl.BlockSpec(memory_space=pltpu.VMEM)
    hbm = pl.BlockSpec(memory_space=pl.ANY)
    chips = SIDE * SIDE
    return pl.pallas_call(
        functools.partial(scatter_kernel, n, wide // 2),
        name="scatter",
        out_shape=(
            jax.ShapeDtypeStruct((tokens, per), BF16),
            jax.ShapeDtypeStruct((128, inner), BF16),
            jax.ShapeDtypeStruct((128, maps), BF16),
            jax.ShapeDtypeStruct((128, heads), BF16),
            jax.ShapeDtypeStruct(sums.shape, F32),
        ),
        in_specs=[hbm, hbm, vm, vm, vm],
        out_specs=(vm,) * 5,
        scratch_shapes=[
            pltpu.VMEM(hidden.shape, BF16),
            pltpu.VMEM((n, rows, 128), BF16),
            pltpu.VMEM((rows, tokens), BF16),
            pltpu.VMEM((SIDE, tokens, per), BF16),
            pltpu.VMEM((tokens, per), BF16),
            pltpu.VMEM((2, tokens, per), BF16),
            pltpu.VMEM((chips, rows, 128), BF16),
            pltpu.VMEM((chips, rows, 128), BF16),
            pltpu.VMEM((chips, rows, 128), BF16),
            pltpu.VMEM((SIDE + 1, rows, 128), BF16),
            pltpu.VMEM((SIDE + 1, 2, rows, 128), BF16),
            pltpu.VMEM((n,) + sums.shape, F32),
            pltpu.SemaphoreType.DMA((chips,)),
            pltpu.SemaphoreType.DMA((chips,)),
            pltpu.SemaphoreType.DMA((36,)),
            pltpu.SemaphoreType.DMA((36,)),
            pltpu.SemaphoreType.DMA((n,)),
            pltpu.SemaphoreType.DMA((n,)),
            pltpu.SemaphoreType.DMA((SIDE + 1,)),
        ],
        compiler_params=pltpu.CompilerParams(
            collective_id=4, has_side_effects=True, vmem_limit_bytes=62 * 2**20
        ),
    )(hidden, w_all, gcols, gdt, sums)


def body(n, hidden, positions, w_x, w_bc, w_dt, a_log, dt_bias, d_skip, grad_out):
    pairs = [(i, i + 1) for i in range(n - 1)]
    earlier = lax.ppermute(positions[-1:], "seq", pairs)
    gap = (positions - jnp.concatenate([earlier, positions[:-1]])).astype(F32)[None, :]
    rate = jnp.exp(a_log)[:, None]
    proj, dtp, w_all = gather_call(n, hidden, w_x, w_bc, w_dt, dt_bias[:, None])
    gcols, gdt, sums = scan_call(n, proj, dtp, gap, rate, d_skip[:, None], grad_out)
    d_hidden, d_w_x, d_w_bc, d_w_dt, totals = scatter_call(n, hidden, w_all, gcols, gdt, sums)
    return d_hidden, d_w_x, d_w_bc, d_w_dt, totals[:, :3].T


def solution(mesh):
    return jax.shard_map(
        functools.partial(body, mesh.shape["seq"]),
        mesh=mesh,
        in_specs=(
            P("seq", None),
            P("seq"),
            P("seq", "head"),
            P("seq", "head"),
            P("seq", "head"),
            P("head"),
            P("head"),
            P("head"),
            P("seq", "head"),
        ),
        out_specs=(
            P("seq", "head"),
            P("seq", "head"),
            P("seq", "head"),
            P("seq", "head"),
            P(None, "head"),
        ),
        check_vma=False,
    )
```

```python
import functools

import jax
import jax.numpy as jnp
from jax import lax
from jax.experimental import pallas as pl
from jax.experimental.pallas import tpu as pltpu
from jax.sharding import PartitionSpec as P

STATE = 128
HEAD_DIM = 64
TILE = 256
LOG2E = 1.4426950408889634
MESH = pl.DeviceIdType.MESH
F32 = jnp.float32
BF16 = jnp.bfloat16
EXACT = lax.Precision.HIGHEST


def dot(a, b, dims, precision=None):
    return lax.dot_general(a, b, (dims, ((), ())), precision=precision, preferred_element_type=F32)


NN = ((1,), (0,))
NT = ((1,), (1,))
TN = ((0,), (0,))


def split2(v):
    hi = v.astype(BF16)
    return hi, (v - hi.astype(F32)).astype(BF16)


def split3(v):
    hi = v.astype(BF16)
    rest = v - hi.astype(F32)
    mid = rest.astype(BF16)
    return hi, mid, (rest - mid.astype(F32)).astype(BF16)


def spread(v, pick):
    parts = split3(v)
    return dot(jnp.concatenate(parts, axis=0), jnp.concatenate([pick] * 3, axis=0), TN)


def gather_heads(pick, y):
    hi, lo = split2(y)
    return dot(pick, hi, NT) + dot(pick, lo, NT)


def picker(heads, width):
    row = lax.broadcasted_iota(jnp.int32, (heads, heads * width), 0)
    col = lax.broadcasted_iota(jnp.int32, (heads, heads * width), 1)
    return jnp.where(col // width == row, 1.0, 0.0).astype(BF16)


def upright(row, size):
    at = lax.broadcasted_iota(jnp.int32, (size, size), 0)
    of = lax.broadcasted_iota(jnp.int32, (size, size), 1)
    return jnp.sum(jnp.where(at == of, row, 0.0), axis=1, keepdims=True)


def sigmoid(v):
    return 1.0 / (1.0 + jnp.exp(-v))


def scan_kernel(
    n,
    pr_ref,
    dtp_ref,
    gap_ref,
    rate_ref,
    skip_ref,
    g_ref,
    gcols_ref,
    gdt_ref,
    sums_ref,
    pay,
    got,
    back,
    home,
    decs,
    dgot,
    xs_ref,
    tail_ref,
    dtx_ref,
    xd_ref,
    xt_ref,
    ge_ref,
    u_ref,
    colb_ref,
    cumt_ref,
    cbt_ref,
    dcbt_ref,
    rowe_ref,
    cole_ref,
    gbc_ref,
    send1,
    recv1,
    send2,
    recv2,
    send3,
    recv3,
):
    tokens = pr_ref.shape[0]
    width = pr_ref.shape[1] - 2 * STATE
    heads = dtp_ref.shape[0]
    blocks = tokens // TILE
    piece = width // n
    me = lax.axis_index("seq")

    barrier = pltpu.get_barrier_semaphore()

    def greet(k, carry):
        pl.semaphore_signal(
            barrier, inc=1, device_id={"seq": lax.rem(me + k, n)}, device_id_type=MESH
        )
        return carry

    lax.fori_loop(1, n, greet, 0)

    pick = picker(heads, HEAD_DIM)
    dtp = dtp_ref[...]
    dt = jnp.maximum(dtp, 0.0) + jnp.log1p(jnp.exp(-jnp.abs(dtp)))
    rate = jnp.exp(upright(rate_ref[...], heads))
    gap = gap_ref[...]
    decay = -rate * dt * gap
    before = lax.broadcasted_iota(jnp.int32, (tokens, tokens), 0)
    after = lax.broadcasted_iota(jnp.int32, (tokens, tokens), 1)
    upto = jnp.where(before <= after, 1.0, 0.0).astype(BF16)
    parts = jnp.concatenate(split3(decay * LOG2E), axis=0)
    raw = dot(parts, upto, NN)
    cum = raw[:heads] + raw[heads : 2 * heads] + raw[2 * heads :]
    cumt_ref[...] = cum
    last = cum[:, tokens - 1 :]
    whole = jnp.exp2(last)
    ecum = jnp.exp2(cum)
    tail = jnp.exp2(last - cum)

    def prepare(b, carry):
        rows = pl.ds(pl.multiple_of(b * TILE, TILE), TILE)
        xp = pr_ref[rows, :width]
        xs = xp * sigmoid(xp)
        xs_ref[rows, :] = xs
        xt_ref[rows, :] = (xs * xd32_ref[rows, :]).astype(BF16)
        ge_ref[rows, :] = (g_ref[rows, :].astype(F32) * u_ref[rows, :]).astype(BF16)
        return carry

    xd32_ref = tail_ref
    xd32_ref[...] = spread(tail * dt, pick)
    u_ref[...] = spread(ecum, pick)
    lax.fori_loop(0, blocks, prepare, 0)
    b_low = pr_ref[:, width : width + STATE].astype(BF16)
    c_low = pr_ref[:, width + STATE :].astype(BF16)
    decs[:, 0, :] = jnp.broadcast_to(whole, (heads, STATE))
    local_state = dot(xt_ref[...], b_low, TN).astype(BF16)
    local_adjoint = dot(ge_ref[...], c_low, TN).astype(BF16)
    pay[:, :piece, :] = local_state.reshape(n, piece, STATE)
    pay[:, piece:, :] = local_adjoint.reshape(n, piece, STATE)
    per_head = n // heads
    got[me] = pay[me]
    dgot[me] = decs[me // per_head]
    pl.semaphore_wait(barrier, n - 1)

    def out_copy(k):
        to = lax.rem(me + k, n)
        return pltpu.make_async_remote_copy(
            pay.at[to], got.at[me], send1.at[k], recv1.at[k], {"seq": to}, MESH
        )

    def dec_copy(k):
        to = lax.rem(me + k, n)
        return pltpu.make_async_remote_copy(
            decs.at[to // per_head], dgot.at[me], send3.at[k], recv3.at[k], {"seq": to}, MESH
        )

    def start_out(k, carry):
        out_copy(k).start()
        dec_copy(k).start()
        return carry

    lax.fori_loop(1, n, start_out, 0)

    colb_ref[...] = spread(cum, picker(heads, 128))
    dtx_ref[...] = spread(dt, pick)
    tail_ref[...] = spread(tail, pick)

    def prepare_more(b, total):
        rows = pl.ds(pl.multiple_of(b * TILE, TILE), TILE)
        xs = xs_ref[rows, :]
        xd_ref[rows, :] = (xs * dtx_ref[rows, :]).astype(BF16)
        dots = gather_heads(pick, g_ref[rows, :].astype(F32) * xs)
        return total + jnp.sum(dots, axis=1, keepdims=True)

    sums_skip = lax.fori_loop(0, blocks, prepare_more, jnp.zeros((heads, 1), F32))
    for i in range(blocks):
        for j in range(i, blocks):
            cbt_ref[i, j] = dot(
                b_low[i * TILE : (i + 1) * TILE], c_low[j * TILE : (j + 1) * TILE], NT
            )
            dcbt_ref[i, j] = jnp.zeros((TILE, TILE), F32)
    cole_ref[...] = jnp.zeros_like(cole_ref)
    s_at = lax.broadcasted_iota(jnp.int32, (TILE, TILE), 0)
    t_at = lax.broadcasted_iota(jnp.int32, (TILE, TILE), 1)
    lane = lax.broadcasted_iota(jnp.int32, (TILE, 128), 1)

    def pair(q, carry):
        cols = pl.ds(pl.multiple_of(q * 128, 128), 128)
        rowe = [[jnp.zeros((1, TILE), F32) for _ in range(blocks)] for _ in range(2)]
        for i in range(blocks):
            srows = pl.ds(i * TILE, TILE)
            xd = xd_ref[srows, cols]
            us = []
            for side in range(2):
                h = q * 2 + side
                lanes = slice(side * HEAD_DIM, (side + 1) * HEAD_DIM)
                col = colb_ref[srows, pl.ds(pl.multiple_of(h * 128, 128), 128)]
                col = jnp.concatenate([col] * (TILE // 128), axis=1)
                u = jnp.zeros((TILE, HEAD_DIM), F32)
                cole = jnp.zeros((TILE, 1), F32)
                for j in range(i, blocks):
                    g = g_ref[pl.ds(j * TILE, TILE), cols][:, lanes]
                    diff = cumt_ref[pl.ds(h, 1), pl.ds(j * TILE, TILE)] - col
                    if i == j:
                        diff = jnp.where(t_at >= s_at, diff, -jnp.inf)
                    within = jnp.exp2(diff)
                    f = within * dot(xd[:, lanes], g, NT)
                    dcbt_ref[i, j] += f
                    cb = cbt_ref[i, j]
                    e = cb * f
                    rowe[side][j] += jnp.sum(e, axis=0, keepdims=True)
                    cole += jnp.sum(e, axis=1, keepdims=True)
                    u += dot((within * cb).astype(BF16), g, NN)
                us.append(u)
                cole_ref[srows, :] = jnp.where(lane == h, cole, cole_ref[srows, :])
            u_ref[srows, cols] = jnp.concatenate(us, axis=1)
        for side in range(2):
            rowe_ref[pl.ds(q * 2 + side, 1), :] = jnp.concatenate(rowe[side], axis=1)
        return carry

    pairs = heads // 2
    lax.fori_loop(0, pairs // 2, pair, 0)

    def wait_out(k, carry):
        out_copy(k).wait_recv()
        dec_copy(k).wait_recv()
        return carry

    lax.fori_loop(1, n, wait_out, 0)

    def decay_of(d):
        return dgot[d]

    def ahead(d, state):
        back[d, :piece, :] = state.astype(BF16)
        return decay_of(d) * state + got[d, :piece, :].astype(F32)

    def behind(k, state):
        d = n - 1 - k
        back[d, piece:, :] = state.astype(BF16)
        return decay_of(d) * state + got[d, piece:, :].astype(F32)

    zero = jnp.zeros((piece, STATE), F32)
    lax.fori_loop(0, n, ahead, zero)
    lax.fori_loop(0, n, behind, zero)
    home[me] = back[me]

    def back_copy(k):
        to = lax.rem(me + k, n)
        return pltpu.make_async_remote_copy(
            back.at[to], home.at[me], send2.at[k], recv2.at[k], {"seq": to}, MESH
        )

    def start_back(k, carry):
        back_copy(k).start()
        return carry

    lax.fori_loop(1, n, start_back, 0)
    lax.fori_loop(pairs // 2, pairs, pair, 0)

    for b in range(blocks):
        rows = pl.ds(b * TILE, TILE)
        grad_b = jnp.zeros((TILE, STATE), F32)
        grad_c = jnp.zeros((TILE, STATE), F32)
        for j in range(b, blocks):
            grad_b += dot(dcbt_ref[b, j].astype(BF16), c_low[j * TILE : (j + 1) * TILE], NN)
        for i in range(b + 1):
            grad_c += dot(dcbt_ref[i, b].astype(BF16), b_low[i * TILE : (i + 1) * TILE], TN)
        gbc_ref[rows, :STATE] = grad_b
        gbc_ref[rows, STATE:] = grad_c
    gcum = rowe_ref[...] - cole_ref[...].T[:heads]
    skip = jnp.broadcast_to(upright(skip_ref[...], heads), (heads, 128))
    skipx = spread(skip, pick)[0:1]

    def wait_back(k, carry):
        back_copy(k).wait_recv()
        back_copy(k).wait_send()
        out_copy(k).wait_send()
        dec_copy(k).wait_send()
        return carry

    lax.fori_loop(1, n, wait_back, 0)

    s_in = home[:, :piece, :].reshape(width, STATE)
    d_out = home[:, piece:, :].reshape(width, STATE)
    grad_dt_parts, r_parts, off_parts = [], [], []
    for b in range(blocks):
        rows = pl.ds(b * TILE, TILE)
        bb, cc = b_low[b * TILE : (b + 1) * TILE], c_low[b * TILE : (b + 1) * TILE]
        tq = tail_ref[rows, :] * dot(bb, d_out, NT)
        z = u_ref[rows, :] + tq
        xs = xs_ref[rows, :]
        grad_dt_parts.append(gather_heads(pick, xs * z))
        r_parts.append(gather_heads(pick, xs * tq))
        off_parts.append(gather_heads(pick, ge_ref[rows, :].astype(F32) * dot(cc, s_in, NT)))
        grad_x = dtx_ref[rows, :] * z + skipx * g_ref[rows, :].astype(F32)
        xp = pr_ref[rows, :width]
        sig = sigmoid(xp)
        gcols_ref[rows, :width] = (grad_x * (sig + xp * sig * (1.0 - sig))).astype(BF16)
        grad_b = gbc_ref[rows, :STATE] + dot(xt_ref[rows, :], d_out, NN)
        grad_c = gbc_ref[rows, STATE:] + dot(ge_ref[rows, :], s_in, NN)
        gcols_ref[rows, width : width + STATE] = grad_b.astype(BF16)
        gcols_ref[rows, width + STATE :] = grad_c.astype(BF16)
    grad_dt = jnp.concatenate(grad_dt_parts, axis=1)
    r = dt * jnp.concatenate(r_parts, axis=1)
    gcum += jnp.concatenate(off_parts, axis=1) - r
    both = jnp.sum(s_in.astype(F32) * d_out.astype(F32), axis=1, keepdims=True)
    both = jnp.broadcast_to(both, (width, 128))
    hi, lo = split2(both)
    both = (dot(pick, hi, NN) + dot(pick, lo, NN))[:, :1]
    at_end = jnp.sum(r, axis=1, keepdims=True) + whole * both
    parts = jnp.concatenate(split3(gcum), axis=0)
    raw = dot(parts, upto, NT)
    grad_decay = raw[:heads] + raw[heads : 2 * heads] + raw[2 * heads :] + at_end
    grad_dt_pre = (grad_dt - grad_decay * rate * gap) * sigmoid(dtp)
    gdt_ref[...] = grad_dt_pre.astype(BF16)
    slot = lax.broadcasted_iota(jnp.int32, (heads, 128), 1)
    sum_a = jnp.sum(grad_decay * decay, axis=1, keepdims=True)
    sum_b = jnp.sum(grad_dt_pre, axis=1, keepdims=True)
    sums_ref[...] = jnp.where(slot == 0, sum_a, jnp.where(slot == 1, sum_b, sums_skip))


def scan_call(n, proj, dtp, gap, rate, skip, g):
    tokens, width = g.shape
    heads = dtp.shape[0]
    blocks = tokens // TILE
    piece = width // n
    vm = pl.BlockSpec(memory_space=pltpu.VMEM)
    return pl.pallas_call(
        functools.partial(scan_kernel, n),
        name="scan",
        out_shape=(
            jax.ShapeDtypeStruct((tokens, width + 2 * STATE), BF16),
            jax.ShapeDtypeStruct((heads, tokens), BF16),
            jax.ShapeDtypeStruct((heads, 128), F32),
        ),
        in_specs=[vm] * 6,
        out_specs=(vm, vm, vm),
        scratch_shapes=[
            pltpu.VMEM((n, 2 * piece, STATE), BF16),
            pltpu.VMEM((n, 2 * piece, STATE), BF16),
            pltpu.VMEM((n, 2 * piece, STATE), BF16),
            pltpu.VMEM((n, 2 * piece, STATE), BF16),
            pltpu.VMEM((heads, 1, STATE), F32),
            pltpu.VMEM((n, 1, STATE), F32),
            pltpu.VMEM((tokens, width), F32),
            pltpu.VMEM((tokens, width), F32),
            pltpu.VMEM((tokens, width), F32),
            pltpu.VMEM((tokens, width), BF16),
            pltpu.VMEM((tokens, width), BF16),
            pltpu.VMEM((tokens, width), BF16),
            pltpu.VMEM((tokens, width), F32),
            pltpu.VMEM((tokens, heads * 128), F32),
            pltpu.VMEM((heads, tokens), F32),
            pltpu.VMEM((blocks, blocks, TILE, TILE), F32),
            pltpu.VMEM((blocks, blocks, TILE, TILE), F32),
            pltpu.VMEM((heads, tokens), F32),
            pltpu.VMEM((tokens, 128), F32),
            pltpu.VMEM((tokens, 2 * STATE), F32),
            pltpu.SemaphoreType.DMA((n,)),
            pltpu.SemaphoreType.DMA((n,)),
            pltpu.SemaphoreType.DMA((n,)),
            pltpu.SemaphoreType.DMA((n,)),
            pltpu.SemaphoreType.DMA((n,)),
            pltpu.SemaphoreType.DMA((n,)),
        ],
        compiler_params=pltpu.CompilerParams(
            collective_id=1, has_side_effects=True, vmem_limit_bytes=60 * 2**20
        ),
    )(proj, dtp, gap, rate, skip, g)


SIDE = 4


def place(n):
    me = lax.axis_index("seq")
    core = lax.rem(me, 2)
    chip = me // 2
    y, z = chip // SIDE, lax.rem(chip, SIDE)
    p = y * (1 - core) + z * core
    q = z * (1 - core) + y * core

    def chip_at(dp, dq):
        return lax.rem(p + dp, SIDE) * (SIDE - (SIDE - 1) * core) + lax.rem(q + dq, SIDE) * (
            1 + (SIDE - 1) * core
        )

    return me, core, chip_at


def greet_all(barrier, ids):
    for axis, to in ids:
        pl.semaphore_signal(barrier, inc=1, device_id={axis: to}, device_id_type=MESH)


def gather_kernel(
    n,
    cut,
    hid_hbm,
    wx_ref,
    wbc_ref,
    wdt_ref,
    bias_ref,
    pos_ref,
    proj_ref,
    dtp_ref,
    gap_ref,
    w_hbm,
    wall,
    hid,
    prev,
    send,
    recv,
    local,
):
    me, core, chip_at = place(n)
    partner = me + 1 - 2 * core
    inner, maps = wx_ref.shape[1], wbc_ref.shape[1]
    wide = inner + maps
    heads = wdt_ref.shape[0]
    rows_all = wide + heads
    after = lax.rem(me + 1, n)

    def sid(dp, dq):
        return 2 * chip_at(dp, dq) + core

    barrier = pltpu.get_barrier_semaphore()
    to_p = (sid(1, 0), sid(3, 0))
    to_q = (sid(0, 1), sid(0, 3))
    around = to_p + to_q + (partner, after, lax.rem(me + n - 1, n))
    greet_all(barrier, [("seq", d) for d in around])
    load = pltpu.make_async_copy(hid_hbm, hid, local.at[n // 2])
    load.start()
    wall[me, :inner, :] = wx_ref[...].T
    wall[me, inner:wide, :] = wbc_ref[...].T
    wall[me, wide:, :] = wdt_ref[...]
    halves = (pl.ds(0, cut), pl.ds(cut, rows_all - cut))
    pl.semaphore_wait(barrier, len(around))

    sent = []

    def copy(slot, half, to, sem):
        ref = wall.at[slot, halves[half]]
        return pltpu.make_async_remote_copy(
            ref, ref, send.at[sem], recv.at[2 * slot + half], {"seq": to}, MESH
        )

    def push(slot, half, to):
        c = copy(slot, half, to, len(sent))
        c.start()
        sent.append(c)

    def arrive(slot, half):
        copy(slot, half, partner, 0).wait_recv()

    for half in range(2):
        push(me, half, to_q[0])
        push(me, 1 - half, to_q[1])
        push(me, half, to_p[0])
        push(me, 1 - half, to_p[1])
    for half in range(2):
        push(me, half, partner)
    place_copy = pltpu.make_async_remote_copy(
        pos_ref, prev, local.at[n // 2 + 1], local.at[n // 2 + 2], {"seq": after}, MESH
    )
    place_copy.start()

    def out_copy(chip):
        return pltpu.make_async_copy(
            wall.at[pl.ds(2 * chip, 2)], w_hbm.at[pl.ds(2 * chip, 2)], local.at[chip]
        )

    def take(dp, dq, first=False):
        chip = chip_at(dp, dq)
        other = 2 * chip + 1 - core
        for half in range(2):
            arrive(other, half)
        out_copy(chip).start()
        a = hid[:, pl.ds(pl.multiple_of(chip * 256, 256), 256)]
        b = jnp.concatenate([wall[2 * chip], wall[2 * chip + 1]], axis=1)
        x, t = dot(a, b[:wide], NT), dot(b[wide:], a, NT)
        if first:
            proj_ref[...] = x
            dtp_ref[...] = t + upright(bias_ref[...], heads)
        else:
            proj_ref[...] += x
            dtp_ref[...] += t

    def takes(count, chip):
        def one(k, carry):
            take(*chip(k))
            return carry

        lax.fori_loop(0, count, one, 0)

    def row_block(dp, half, forward=None):
        slot = sid(dp, 0)
        arrive(slot, half)
        if forward is not None:
            push(slot, half, to_p[forward])
        push(slot, half, to_q[0])
        push(slot, half, to_q[1])
        push(slot, half, partner)

    def onward(dp):
        for side, dq in enumerate((3, 1)):
            slot = sid(dp, dq)
            arrive(slot, side)
            push(slot, side, to_q[side])
            push(slot, side, partner)

    def rest(dp):
        for side, dq in enumerate((3, 1)):
            slot = sid(dp, dq)
            arrive(slot, 1 - side)
            push(slot, 1 - side, partner)

    def opposite(dp):
        for half in range(2):
            slot = sid(dp, 2)
            arrive(slot, half)
            push(slot, half, partner)

    load.wait()
    take(0, 0, True)
    row_block(3, 0, 0)
    row_block(1, 1, 1)
    onward(0)
    row_block(3, 1)
    row_block(1, 0)
    rest(0)
    takes(4, lambda k: ((1 - k // 2) * (1 + 2 * lax.rem(k, 2)), (k // 2) * (1 + 2 * lax.rem(k, 2))))
    row_block(2, 0)
    row_block(2, 1)
    onward(3)
    onward(1)
    opposite(0)
    takes(2, lambda k: (2 * k, 2 - 2 * k))
    rest(3)
    rest(1)
    onward(2)
    takes(4, lambda k: (1 + 2 * lax.rem(k, 2), 1 + 2 * (k // 2)))
    rest(2)
    opposite(3)
    opposite(1)
    takes(
        4,
        lambda k: (
            2 * (1 - k // 2) + (1 + 2 * lax.rem(k, 2)) * (k // 2),
            (1 + 2 * lax.rem(k, 2)) * (1 - k // 2) + 2 * (k // 2),
        ),
    )
    opposite(2)
    take(2, 2)

    place_copy.wait()
    tokens = pos_ref.shape[1]
    here = jnp.broadcast_to(pos_ref[...].astype(F32), (8, tokens))
    there = jnp.broadcast_to(prev[...].astype(F32), (8, tokens))
    there = jnp.where(me == 0, 0.0, pltpu.roll(there, 1, 1))
    lane = lax.broadcasted_iota(jnp.int32, (8, tokens), 1)
    gap_ref[...] = (here - jnp.where(lane == 0, there, pltpu.roll(here, 1, 1)))[0:1]
    for c in sent:
        c.wait_send()

    def stored(k, carry):
        out_copy(k).wait()
        return carry

    lax.fori_loop(0, n // 2, stored, 0)


def gather_call(n, hidden, w_x, w_bc, w_dt, bias, positions):
    tokens = hidden.shape[0]
    heads = w_dt.shape[0]
    wide = w_x.shape[1] + w_bc.shape[1]
    rows = wide + heads
    vm = pl.BlockSpec(memory_space=pltpu.VMEM)
    hbm = pl.BlockSpec(memory_space=pl.ANY)
    return pl.pallas_call(
        functools.partial(gather_kernel, n, wide // 2),
        name="gather",
        out_shape=(
            jax.ShapeDtypeStruct((tokens, wide), F32),
            jax.ShapeDtypeStruct((heads, tokens), F32),
            jax.ShapeDtypeStruct((1, tokens), F32),
            jax.ShapeDtypeStruct((n, rows, 128), BF16),
        ),
        in_specs=[hbm, vm, vm, vm, vm, vm],
        out_specs=(vm, vm, vm, hbm),
        scratch_shapes=[
            pltpu.VMEM((n, rows, 128), BF16),
            pltpu.VMEM(hidden.shape, BF16),
            pltpu.VMEM(positions.shape, positions.dtype),
            pltpu.SemaphoreType.DMA((62,)),
            pltpu.SemaphoreType.DMA((2 * n,)),
            pltpu.SemaphoreType.DMA((n // 2 + 3,)),
        ],
        compiler_params=pltpu.CompilerParams(
            collective_id=3, has_side_effects=True, vmem_limit_bytes=60 * 2**20
        ),
    )(hidden, w_x, w_bc, w_dt, bias, positions)


class Ring:
    def __init__(self, axis, ids, cut, total, send, recv, base):
        self.axis, self.ids, self.base = axis, ids, base
        self.send, self.recv = send, recv
        self.rows = (pl.ds(0, cut), pl.ds(cut, total - cut))

    def bind(self, blocks, rel, fin):
        self.blocks, self.rel, self.fin = blocks, rel, fin
        low, high = self.rows
        plan = (
            (2, low, rel.at[low], 0),
            (2, high, rel.at[high], 1),
            (1, high, fin.at[0, high], 0),
            (3, low, fin.at[1, low], 1),
            (1, low, fin.at[0, low], 0),
            (3, high, fin.at[1, high], 1),
        )
        self.copies = [
            pltpu.make_async_remote_copy(
                blocks[b].at[rows],
                dst,
                self.send.at[self.base + k],
                self.recv.at[self.base + k],
                {self.axis: self.ids[side]},
                MESH,
            )
            for k, (b, rows, dst, side) in enumerate(plan)
        ]
        return self

    def relay(self):
        for k, (b, rows) in enumerate(((1, self.rows[0]), (3, self.rows[1]))):
            self.copies[k].wait_recv()
            ref = self.blocks[b]
            ref[rows, :] = (ref[rows, :].astype(F32) + self.rel[rows, :].astype(F32)).astype(BF16)
            self.copies[4 + k].start()

    def final(self):
        for k in range(2, 6):
            self.copies[k].wait_recv()
        own = self.blocks[0][...].astype(F32)
        return own + self.fin[0].astype(F32) + self.fin[1].astype(F32)

    def drain(self):
        for c in self.copies:
            c.wait_send()


def scatter_kernel(
    n,
    cut,
    hid_hbm,
    w_hbm,
    g_ref,
    gdt_ref,
    sums_ref,
    dh_ref,
    dwx_ref,
    dwbc_ref,
    dwdt_ref,
    tot_ref,
    hid,
    w,
    gt,
    xbuf,
    xrel,
    xfin,
    mine,
    theirs,
    fromp,
    rel,
    fin,
    got,
    send_p,
    recv_p,
    send_r,
    recv_r,
    send_s,
    recv_s,
    local,
):
    me, core, chip_at = place(n)
    partner = me + 1 - 2 * core
    head = lax.axis_index("head")
    tokens, wide = g_ref.shape
    inner = dwx_ref.shape[1]
    rows_all = gt.shape[0]
    per = n // SIDE

    def sid(dp, dq):
        return 2 * chip_at(dp, dq) + core

    def at_head(d):
        return lax.rem(head + d, SIDE)

    barrier = pltpu.get_barrier_semaphore()
    x_ids = (at_head(1), at_head(3))

    def greet(k, carry):
        pl.semaphore_signal(
            barrier, inc=1, device_id={"seq": lax.rem(me + k, n)}, device_id_type=MESH
        )
        return carry

    lax.fori_loop(1, n, greet, 0)
    greet_all(barrier, [("head", d) for d in x_ids])

    def w_copy(d):
        part = pl.ds(at_head(d) * per, per)
        return pltpu.make_async_copy(w_hbm.at[part], w.at[part], local.at[d])

    w_copy(2).start()
    load = pltpu.make_async_copy(hid_hbm, hid, local.at[SIDE])
    load.start()
    for d in (1, 3, 0):
        w_copy(d).start()
    gt[:wide, :] = g_ref[...].T
    gt[wide:, :] = gdt_ref[...]

    x_ring = Ring("head", x_ids, tokens // 2, tokens, send_r, recv_r, 0).bind(
        [xbuf.at[d] for d in range(SIDE)], xrel, xfin
    )
    q_ids = (sid(0, 1), sid(0, 3))
    p_ids = (sid(1, 0), sid(3, 0))
    groups = {}
    for a in range(SIDE):
        groups[a] = Ring("seq", q_ids, cut, rows_all, send_r, recv_r, 6 + 6 * a).bind(
            [mine.at[a * SIDE + b] for b in range(SIDE)], rel.at[a], fin.at[a]
        )
    p_ring = Ring("seq", p_ids, cut, rows_all, send_r, recv_r, 30).bind(
        [mine.at[a * SIDE] for a in range(SIDE)], rel.at[SIDE], fin.at[SIDE]
    )

    def hidden_part(d):
        first = at_head(d) * per

        def one(k, carry):
            b = jnp.concatenate([w[first + 2 * k], w[first + 2 * k + 1]], axis=1)
            part = dot(g_ref[...], b[:wide], NN) + dot(gdt_ref[...], b[wide:], TN)
            xbuf[d, :, pl.ds(pl.multiple_of(k * 256, 256), 256)] = part.astype(BF16)
            return carry

        lax.fori_loop(0, per // 2, one, 0)

    def partner_copy(a, b):
        return pltpu.make_async_remote_copy(
            theirs.at[a * SIDE + b],
            fromp.at[b * SIDE + a],
            send_p.at[a * SIDE + b],
            recv_p.at[b * SIDE + a],
            {"seq": partner},
            MESH,
        )

    def weight_part(a, b):
        chip = chip_at(a, b)
        at = a * SIDE + b
        x = jnp.concatenate(
            [
                hid[:, pl.ds(pl.multiple_of(chip * 256 + 128 * core, 128), 128)],
                hid[:, pl.ds(pl.multiple_of(chip * 256 + 128 * (1 - core), 128), 128)],
            ],
            axis=1,
        )
        part = dot(gt[...], x, NN).astype(BF16)
        mine[at] = part[:, :128]
        theirs[at] = part[:, 128:]
        partner_copy(a, b).start()

    def weights(count, chip):
        def one(k, carry):
            weight_part(*chip(k))
            return carry

        lax.fori_loop(0, count, one, 0)

    def pairs(a, first, step, count):
        def one(k, carry):
            b = first + k * step
            at = a * SIDE + b
            partner_copy(b, a).wait_recv()
            mine[at] = (mine[at].astype(F32) + fromp[at].astype(F32)).astype(BF16)
            return carry

        lax.fori_loop(0, count, one, 0)

    def start(ring, *kinds):
        for k in kinds:
            ring.copies[k].start()

    def line_sum(a):
        mine[a * SIDE] = groups[a].final().astype(BF16)

    def sums_copy(k):
        to = lax.rem(me + k, n)
        return pltpu.make_async_remote_copy(
            sums_ref, got.at[me], send_s.at[k], recv_s.at[k], {"seq": to}, MESH
        )

    def near(k):
        return 1 + 2 * lax.rem(k, 2)

    w_copy(2).wait()
    hidden_part(2)
    pl.semaphore_wait(barrier, n + 1)
    start(x_ring, 0, 1)
    load.wait()
    weight_part(2, 2)
    weight_part(1, 2)
    weight_part(2, 1)
    pairs(2, 2, 1, 1)
    start(groups[2], 0, 1)
    pairs(1, 2, 1, 1)
    start(groups[1], 0, 1)
    weight_part(3, 2)
    weight_part(2, 3)
    pairs(3, 2, 1, 1)
    start(groups[3], 0, 1)
    pairs(2, 1, 2, 2)
    start(groups[2], 2, 3)
    weights(4, lambda k: (near(k), near(k // 2)))
    groups[2].relay()
    pairs(1, 1, 2, 2)
    start(groups[1], 2, 3)
    pairs(3, 1, 2, 2)
    start(groups[3], 2, 3)
    w_copy(1).wait()
    w_copy(3).wait()
    hidden_part(1)
    start(x_ring, 2)
    hidden_part(3)
    start(x_ring, 3)
    weights(2, lambda k: (2 * k, 2 - 2 * k))
    groups[1].relay()
    groups[3].relay()
    pairs(0, 2, 1, 1)
    start(groups[0], 0, 1)
    weights(4, lambda k: (near(k) * (k // 2), near(k) * (1 - k // 2)))
    x_ring.relay()
    pairs(0, 1, 2, 2)
    start(groups[0], 2, 3)
    pairs(2, 0, 1, 1)
    line_sum(2)
    start(p_ring, 0, 1)
    groups[0].relay()
    weight_part(0, 0)
    w_copy(0).wait()
    hidden_part(0)
    pairs(1, 0, 1, 1)
    line_sum(1)
    start(p_ring, 2)
    pairs(3, 0, 1, 1)
    line_sum(3)
    start(p_ring, 3)
    p_ring.relay()

    def start_sums(k, carry):
        sums_copy(k).start()
        return carry

    lax.fori_loop(1, n, start_sums, 0)
    got[me] = sums_ref[...]
    pairs(0, 0, 1, 1)
    line_sum(0)

    def wait_sums(k, carry):
        sums_copy(k).wait()
        return carry

    lax.fori_loop(1, n, wait_sums, 0)
    tot_ref[...] = jnp.sum(got[...], axis=0).T[:3]
    grads = p_ring.final()
    dwx_ref[...] = grads[:inner].T.astype(BF16)
    dwbc_ref[...] = grads[inner:wide].T.astype(BF16)
    dwdt_ref[...] = grads[wide:].astype(BF16)
    dh_ref[...] = x_ring.final().astype(BF16)
    x_ring.drain()
    p_ring.drain()
    for ring in groups.values():
        ring.drain()

    def drained(k, carry):
        partner_copy(k // SIDE, lax.rem(k, SIDE)).wait_send()
        return carry

    lax.fori_loop(0, SIDE * SIDE, drained, 0)


def scatter_call(n, hidden, w_all, gcols, gdt, sums):
    tokens, wide = gcols.shape
    heads = gdt.shape[0]
    maps = 2 * STATE
    inner = wide - maps
    rows = wide + heads
    per = hidden.shape[1] // SIDE
    vm = pl.BlockSpec(memory_space=pltpu.VMEM)
    hbm = pl.BlockSpec(memory_space=pl.ANY)
    chips = SIDE * SIDE
    return pl.pallas_call(
        functools.partial(scatter_kernel, n, wide // 2),
        name="scatter",
        out_shape=(
            jax.ShapeDtypeStruct((tokens, per), BF16),
            jax.ShapeDtypeStruct((128, inner), BF16),
            jax.ShapeDtypeStruct((128, maps), BF16),
            jax.ShapeDtypeStruct((heads, 128), BF16),
            jax.ShapeDtypeStruct((3, heads), F32),
        ),
        in_specs=[hbm, hbm, vm, vm, vm],
        out_specs=(vm,) * 5,
        scratch_shapes=[
            pltpu.VMEM(hidden.shape, BF16),
            pltpu.VMEM((n, rows, 128), BF16),
            pltpu.VMEM((rows, tokens), BF16),
            pltpu.VMEM((SIDE, tokens, per), BF16),
            pltpu.VMEM((tokens, per), BF16),
            pltpu.VMEM((2, tokens, per), BF16),
            pltpu.VMEM((chips, rows, 128), BF16),
            pltpu.VMEM((chips, rows, 128), BF16),
            pltpu.VMEM((chips, rows, 128), BF16),
            pltpu.VMEM((SIDE + 1, rows, 128), BF16),
            pltpu.VMEM((SIDE + 1, 2, rows, 128), BF16),
            pltpu.VMEM((n,) + sums.shape, F32),
            pltpu.SemaphoreType.DMA((chips,)),
            pltpu.SemaphoreType.DMA((chips,)),
            pltpu.SemaphoreType.DMA((36,)),
            pltpu.SemaphoreType.DMA((36,)),
            pltpu.SemaphoreType.DMA((n,)),
            pltpu.SemaphoreType.DMA((n,)),
            pltpu.SemaphoreType.DMA((SIDE + 1,)),
        ],
        compiler_params=pltpu.CompilerParams(
            collective_id=4, has_side_effects=True, vmem_limit_bytes=62 * 2**20
        ),
    )(hidden, w_all, gcols, gdt, sums)


def finish_kernel(*refs):
    half = len(refs) // 2
    for source, result in zip(refs[:half], refs[half:]):
        result[...] = source[...]


def finish_call(*values):
    vm = pl.BlockSpec(memory_space=pltpu.VMEM)
    return pl.pallas_call(
        finish_kernel,
        name="finish",
        out_shape=tuple(jax.ShapeDtypeStruct(v.shape, v.dtype) for v in values),
        in_specs=[vm] * len(values),
        out_specs=(vm,) * len(values),
    )(*values)


def body(n, hidden, positions, w_x, w_bc, w_dt, a_log, dt_bias, d_skip, grad_out):
    proj, dtp, gap, w_all = gather_call(
        n, hidden, w_x, w_bc, w_dt.T, dt_bias[None, :], positions[None, :]
    )
    gcols, gdt, sums = scan_call(
        n, proj, dtp, gap, a_log[None, :], d_skip[None, :], grad_out
    )
    d_hidden, d_w_x, d_w_bc, d_w_dt, d_params = finish_call(
        *scatter_call(n, hidden, w_all, gcols, gdt, sums)
    )
    return d_hidden, d_w_x, d_w_bc, d_w_dt.T, d_params


def solution(mesh):
    return jax.shard_map(
        functools.partial(body, mesh.shape["seq"]),
        mesh=mesh,
        in_specs=(
            P("seq", None),
            P("seq"),
            P("seq", "head"),
            P("seq", "head"),
            P("seq", "head"),
            P("head"),
            P("head"),
            P("head"),
            P("seq", "head"),
        ),
        out_specs=(
            P("seq", "head"),
            P("seq", "head"),
            P("seq", "head"),
            P("seq", "head"),
            P(None, "head"),
        ),
        check_vma=False,
    )
```
